32 devices in a mesh: chan: 2 (over x), row: 4 (over z), col: 4 (over y, core).
Axes of the slice: x: 2, y: 2, z: 4, core: 2. Of those that a mesh axis runs over, the one named last changes fastest.
Arguments:
- voltages: bfloat16 [2, 1024, 131072], P(None, 'chan', ('row', 'col')), may hold values from -6 to 6
- input_flags: int32 [1024], P('chan'), may hold values 0 or 1
- channel_order: int32 [128], replicated, may hold values from 0 to 127, each once
- beam_weights: bfloat16 [2, 128, 256, 1024], P(None, 'chan', 'col'), may hold values from -0.1875 to 0.1875
Outputs:
- visibility: float32 [2, 128, 1024, 1024], P(None, 'chan', 'row', 'col')
- beam_power: float32 [128, 256, 128], P('chan', 'col', 'row')
The draws below stay inside these ranges and needn't reach their ends.
Inputs may be any that keep to these rules, and one draw needn't show every extreme that they name: `channel_order`: every fine channel appears exactly once.
All inputs are finite; a program needn't handle non-finite values. No bound on the sum of `input_flags` on one device may be relied on, other than what follows from the above.
Results may differ from the reference program's by a relative error of at most 0.005.
Values may be sent and summed in bfloat16 or wider, within the bound.
A program may use at most 448 MiB of HBM per device.

```python
import math
import jax
import jax.numpy as jnp
from jax import lax

INPUTS = 1024
NCH = 128
TAPS = 4
BEAMS = 256
INTEG = 8
FRAMES = 1024
BINS = 128


def touch_ends(result, own_key, low, largest):
    index_at = [jax.random.randint(jax.random.fold_in(own_key, axis), (), 0, length) for axis, length in enumerate(result.shape)]
    widest = result.shape.index(max(result.shape))
    neighbour = index_at[:widest] + [(index_at[widest] + 1) % result.shape[widest]] + index_at[widest + 1:]
    return result.at[tuple(index_at)].set(low).at[tuple(neighbour)].set(largest)


def levels(stream_key, shape, pieces, least, largest):
    loudness = 1.0
    for dim, parts in pieces:
        draws = jax.random.uniform(jax.random.fold_in(jax.random.fold_in(stream_key, 6), dim), (parts,), jnp.float32, least / len(pieces), largest / len(pieces))
        loudness = loudness * jnp.repeat(jnp.exp(draws), shape[dim] // parts).reshape((-1,) + (1,) * (len(shape) - 1 - dim))
    return loudness


def normal_values(key, dims, spread, most, pieces=(), kind=jnp.bfloat16):
    level = levels(key, dims, pieces, -0.22, 0.18) if pieces else 1.0
    drawn = jax.random.normal(key, dims, jnp.float32) * spread * level
    return jnp.minimum(jnp.maximum(drawn, -most), most).astype(kind)


def setup_inputs(seed: int = 0) -> dict:
    seeds = jax.random.split(jax.random.key(seed), 5)
    voltages = normal_values(seeds[0], (2, INPUTS, FRAMES * NCH), 1.0, 6.0, ((1, 2), (2, 16)))
    input_flags = touch_ends((jax.random.randint(seeds[1], (INPUTS,), 0, 8) < 7).astype(jnp.int32), jax.random.fold_in(seeds[1], 1), 0, 1)
    channel_order = jax.random.permutation(seeds[2], NCH).astype(jnp.int32)
    beam_weights = normal_values(seeds[3], (2, NCH, BEAMS, INPUTS), INPUTS ** -0.5, 0.1875, ((1, 2), (2, 4)))
    return {"voltages": voltages, "input_flags": input_flags, "channel_order": channel_order, "beam_weights": beam_weights}


def prototype(taps, length):
    position = jnp.arange(taps * length, dtype=jnp.float32) + 0.5
    offset = position / length - taps / 2.0
    window = 0.5 - 0.5 * jnp.cos(2.0 * math.pi * position / (taps * length))
    return (jnp.sin(math.pi * offset) / (math.pi * offset) * window).reshape(taps, length)

def dft_tables(channel_rows, length):
    sample_index = jnp.arange(length, dtype=jnp.int32)
    product = channel_rows[:, None] * sample_index[None, :] % length
    angle = 2.0 * math.pi / length * product.astype(jnp.float32)
    factor = 1.0 / math.sqrt(length)
    cosine = jnp.cos(angle) * factor
    sine = jnp.sin(angle) * factor
    real_rows = jnp.stack([cosine, sine], axis=1)
    imag_rows = jnp.stack([-sine, cosine], axis=1)
    return jnp.stack([real_rows, imag_rows], axis=1).astype(jnp.bfloat16)

def reference(voltages, input_flags, channel_order, beam_weights):
    masked = voltages * input_flags.astype(jnp.bfloat16)[None, :, None]
    padded = jnp.concatenate([jnp.zeros((2, INPUTS, (TAPS - 1) * NCH), jnp.bfloat16), masked], axis=2)
    blocks = padded.reshape(2, INPUTS, FRAMES + TAPS - 1, NCH)
    coeffs = prototype(TAPS, NCH)
    filtered = jnp.zeros((2, INPUTS, FRAMES, NCH), jnp.float32)
    for tap_index in range(TAPS):
        filtered = filtered + coeffs[tap_index] * blocks[:, :, tap_index:tap_index + FRAMES].astype(jnp.float32)
    filtered = filtered.astype(jnp.bfloat16)
    tables = dft_tables(jnp.arange(NCH, dtype=jnp.int32), NCH)
    spectrum = jnp.einsum('kqpn,pifn->kiqf', tables.astype(jnp.float32), filtered.astype(jnp.float32), precision=lax.Precision.HIGHEST).astype(jnp.bfloat16)
    ordered = spectrum[channel_order]
    weights_by_channel = jnp.transpose(beam_weights, (1, 0, 2, 3))

    def per_channel(items):
        block, weights = items
        real_part = block[:, 0].astype(jnp.float32)
        imag_part = block[:, 1].astype(jnp.float32)
        vis_re = (jnp.dot(real_part, real_part.T, precision=lax.Precision.HIGHEST) + jnp.dot(imag_part, imag_part.T, precision=lax.Precision.HIGHEST)) / FRAMES
        vis_im = (jnp.dot(imag_part, real_part.T, precision=lax.Precision.HIGHEST) - jnp.dot(real_part, imag_part.T, precision=lax.Precision.HIGHEST)) / FRAMES
        w_real = weights[0].astype(jnp.float32)
        w_imag = weights[1].astype(jnp.float32)
        beam_re = jnp.dot(w_real, real_part, precision=lax.Precision.HIGHEST) - jnp.dot(w_imag, imag_part, precision=lax.Precision.HIGHEST)
        beam_im = jnp.dot(w_real, imag_part, precision=lax.Precision.HIGHEST) + jnp.dot(w_imag, real_part, precision=lax.Precision.HIGHEST)
        power = beam_re * beam_re + beam_im * beam_im
        binned = power.reshape(BEAMS, BINS, INTEG).mean(axis=-1)
        return (jnp.stack([vis_re, vis_im]), binned)
    vis_all, beam_power = lax.map(per_channel, (ordered, weights_by_channel))
    visibility = jnp.transpose(vis_all, (1, 0, 2, 3))
    return (visibility, beam_power)
```

```python
import functools
import math

import jax
import jax.numpy as jnp
from jax import lax
from jax.experimental import pallas as pl
from jax.experimental.pallas import tpu as pltpu
from jax.sharding import PartitionSpec as P

NCH = 128
TAPS = 4
INTEG = 8


def passed_along(value, axis, steps):
    count = lax.axis_size(axis)
    initial, last = (max(0, -steps), min(count, count - steps))
    return lax.ppermute(value, axis, [(source, source + steps) for source in range(initial, last)])


def prototype(taps, length):
    position = jnp.arange(taps * length, dtype=jnp.float32) + 0.5
    offset = position / length - taps / 2.0
    window = 0.5 - 0.5 * jnp.cos(2.0 * math.pi * position / (taps * length))
    return (jnp.sin(math.pi * offset) / (math.pi * offset) * window).reshape(taps, length)


def dft_tables(channel_rows, length):
    sample_index = jnp.arange(length, dtype=jnp.int32)
    product = channel_rows[:, None] * sample_index[None, :] % length
    angle = 2.0 * math.pi / length * product.astype(jnp.float32)
    factor = 1.0 / math.sqrt(length)
    cosine = jnp.cos(angle) * factor
    sine = jnp.sin(angle) * factor
    real_rows = jnp.stack([cosine, sine], axis=1)
    imag_rows = jnp.stack([-sine, cosine], axis=1)
    return jnp.stack([real_rows, imag_rows], axis=1).astype(jnp.bfloat16)


def to_frames(gathered, frames, outer, inner, swapped):
    chans = gathered.shape[0]
    width = gathered.shape[1]
    split = gathered.reshape(chans, width, outer, inner, 2, frames)
    if swapped:
        order = jnp.transpose(split, (0, 4, 1, 3, 2, 5))
    else:
        order = jnp.transpose(split, (0, 4, 1, 2, 3, 5))
    return order.reshape(chans, 2, width, outer * inner * frames)


def correlate_one(left_block, right_block, frame_count):
    left_re = left_block[0]
    left_im = left_block[1]
    right_re = right_block[0]
    right_im = right_block[1]
    dims = (((1,), (1,)), ((), ()))
    vis_re = lax.dot_general(left_re, right_re, dims, preferred_element_type=jnp.float32)
    vis_re = vis_re + lax.dot_general(left_im, right_im, dims, preferred_element_type=jnp.float32)
    vis_im = lax.dot_general(left_im, right_re, dims, preferred_element_type=jnp.float32)
    vis_im = vis_im - lax.dot_general(left_re, right_im, dims, preferred_element_type=jnp.float32)
    return jnp.stack([vis_re, vis_im]) / frame_count


def correlate(left_view, right_view, frame_count):
    result = lax.map(
        lambda items: correlate_one(items[0], items[1], frame_count), (left_view, right_view)
    )
    return jnp.transpose(result, (1, 0, 2, 3))


def beams_one(weights, block):
    w_real = weights[0]
    w_imag = weights[1]
    x_real = block[0]
    x_imag = block[1]
    beam_re = jnp.dot(w_real, x_real, preferred_element_type=jnp.float32) - jnp.dot(
        w_imag, x_imag, preferred_element_type=jnp.float32
    )
    beam_im = jnp.dot(w_real, x_imag, preferred_element_type=jnp.float32) + jnp.dot(
        w_imag, x_real, preferred_element_type=jnp.float32
    )
    return jnp.stack([beam_re, beam_im], axis=1)


def form_beams(weights, view):
    by_channel = jnp.transpose(weights, (1, 0, 2, 3))
    return lax.map(lambda items: beams_one(items[0], items[1]), (by_channel, view))


def integrate(voltage):
    power = voltage[:, :, 0] * voltage[:, :, 0] + voltage[:, :, 1] * voltage[:, :, 1]
    return power.reshape(power.shape[0], power.shape[1], -1, INTEG).mean(axis=-1)


def channelize(voltages, input_flags, channel_order):
    masked = voltages * input_flags.astype(jnp.bfloat16)[None, :, None]
    local_inputs = masked.shape[1]
    frames = masked.shape[2] // NCH
    history = passed_along(masked[:, :, masked.shape[2] - (TAPS - 1) * NCH :], ("row", "col"), 1)
    joined = jnp.concatenate([history, masked], axis=2)
    blocks = joined.reshape(2, local_inputs, frames + TAPS - 1, NCH)
    coeffs = prototype(TAPS, NCH)
    filtered = jnp.zeros((2, local_inputs, frames, NCH), jnp.float32)
    for tap_index in range(TAPS):
        filtered = filtered + coeffs[tap_index] * blocks[
            :, :, tap_index : tap_index + frames
        ].astype(jnp.float32)
    filtered = filtered.astype(jnp.bfloat16)
    tables = dft_tables(channel_order, NCH)
    spectrum = jnp.einsum(
        "kqpn,pifn->kiqf",
        tables.astype(jnp.float32),
        filtered.astype(jnp.float32),
        precision=lax.Precision.HIGHEST,
    ).astype(jnp.bfloat16)
    spectrum = spectrum.reshape(NCH, local_inputs, 2 * frames)
    return spectrum


def by_panels(voltages, input_flags, channel_order, beam_weights):
    spectrum = channelize(voltages, input_flags, channel_order)
    frames = spectrum.shape[2] // 2
    turned = lax.all_to_all(spectrum, "chan", split_axis=0, concat_axis=1, tiled=True)
    row_count = lax.axis_size("row")
    col_count = lax.axis_size("col")
    total_frames = frames * row_count * col_count
    row_turned = lax.all_to_all(turned, "row", split_axis=1, concat_axis=2, tiled=True)
    row_all = lax.all_gather(row_turned, "col", axis=2, tiled=True)
    col_turned = lax.all_to_all(turned, "col", split_axis=1, concat_axis=2, tiled=True)
    col_all = lax.all_gather(col_turned, "row", axis=2, tiled=True)
    row_view = to_frames(row_all, frames, col_count, row_count, True)
    col_view = to_frames(col_all, frames, row_count, col_count, False)
    visibility = correlate(row_view, col_view, total_frames)
    weights_all = lax.all_gather(beam_weights, "col", axis=2, tiled=True)
    local_view = to_frames(turned, frames, 1, 1, False)
    voltage = form_beams(weights_all, local_view)
    own_power = integrate(voltage)
    beam_power = lax.all_to_all(own_power, "col", split_axis=1, concat_axis=2, tiled=True)
    return (visibility, beam_power)


MESH = pl.DeviceIdType.MESH


def spectra_tile(v_ref, h_ref, flag_ref, coeff_ref, table_ref, filtered_ref, wide_ref):
    tile = v_ref.shape[1]
    frames = v_ref.shape[2] // NCH
    lanes = 2 * frames
    flag = jnp.broadcast_to(flag_ref[...], (tile, NCH))
    rows = [jnp.broadcast_to(coeff_ref[tap : tap + 1, :], (tile, NCH)) for tap in range(TAPS)]
    for part in range(2):

        def frame_at(index):
            ref, at = (h_ref, index) if index < TAPS - 1 else (v_ref, index - TAPS + 1)
            return ref[part, :, at * NCH : (at + 1) * NCH].astype(jnp.float32) * flag

        window = [frame_at(index) for index in range(TAPS - 1)]
        for frame in range(frames):
            window = window[-(TAPS - 1) :] + [frame_at(frame + TAPS - 1)]
            total = rows[0] * window[0]
            for tap in range(1, TAPS):
                total = total + rows[tap] * window[tap]
            filtered_ref[part, frame] = total
    for first in range(0, tile, 2):
        stack = []
        for index in (first, first + 1):
            re = filtered_ref[0, :, index, :].astype(jnp.bfloat16)
            im = filtered_ref[1, :, index, :].astype(jnp.bfloat16)
            stack.append(jnp.concatenate([re, im], axis=1))
            stack.append(jnp.concatenate([im, -re], axis=1))
        both = lax.dot_general(
            table_ref[...],
            jnp.concatenate(stack, axis=0),
            (((1,), (1,)), ((), ())),
            preferred_element_type=jnp.float32,
        )
        wide_ref[:, first, :] = both[:, :lanes]
        wide_ref[:, first + 1, :] = both[:, lanes:]
    return wide_ref[...].astype(jnp.bfloat16)


def sizes():
    return lax.axis_size("chan"), lax.axis_size("row"), lax.axis_size("col")


def turn_kernel(
    cs, rs, qs, tile, group,
    v_ref, h_ref, flag_ref, coeff_ref, table_ref, weight_ref, x_ref, w_ref,
    filtered_ref, wide_ref, spec_ref, send, recv, wsend, wrecv, local,
):
    c, r, q = (lax.axis_index(name) for name in ("chan", "row", "col"))
    cells = rs * qs
    devices = cs * cells
    me = r * qs + q
    here = c * cells + me
    own = spec_ref.shape[0] // devices
    inputs = spec_ref.shape[1]
    lanes = spec_ref.shape[2]
    beams = weight_ref.shape[2]
    turn_step = pl.program_id(0)
    tiles = inputs // tile

    def ahead(step, sign):
        row = (r + rs + sign * (step % rs)) % rs
        return row * qs + (q + qs + sign * (step // rs)) % qs

    def spectra(step, outgoing, first, count):
        if outgoing:
            chan, cell = (c + step % cs) % cs, ahead(step // cs, 1)
            origin, column = c, me
            slot = here
        else:
            chan, cell = (c + cs - step % cs) % cs, ahead(step // cs, -1)
            origin, column = chan, cell
            slot = chan * cells + cell
        return pltpu.make_async_remote_copy(
            src_ref=spec_ref.at[
                pl.ds((chan * cells + cell) * own, own),
                pl.ds(pl.multiple_of(first, tile), count),
            ],
            dst_ref=x_ref.at[
                :,
                pl.ds(pl.multiple_of(origin * inputs + first, tile), count),
                pl.ds(pl.multiple_of(column * lanes, lanes), lanes),
            ],
            send_sem=send.at[chan * cells + cell],
            recv_sem=recv.at[slot],
            device_id=(chan, cell // qs, cell % qs),
            device_id_type=MESH,
        )

    def weights(step, outgoing):
        if outgoing:
            peer = (q + step) % qs
            slot = q
        else:
            peer = (q + qs - step) % qs
            slot = peer
        return pltpu.make_async_remote_copy(
            src_ref=weight_ref.at[:, pl.ds((r * qs + peer) * own, own)],
            dst_ref=w_ref.at[:, :, pl.ds(pl.multiple_of(slot * beams, beams), beams)],
            send_sem=wsend.at[peer],
            recv_sem=wrecv.at[slot],
            device_id=(c, r, peer),
            device_id_type=MESH,
        )

    keep = pltpu.make_async_copy(
        weight_ref.at[:, pl.ds(me * own, own)],
        w_ref.at[:, :, pl.ds(pl.multiple_of(q * beams, beams), beams)],
        local.at[1],
    )

    @pl.when(turn_step == 0)
    def _():
        def start_weights(step, carry):
            weights(step, True).start()
            return carry

        lax.fori_loop(1, qs, start_weights, 0)
        keep.start()

    @pl.when((turn_step > 0) & (turn_step * tile % group == 0))
    def _():
        def start(step, carry):
            spectra(step, True, turn_step * tile - group, group).start()
            return carry

        lax.fori_loop(1, devices, start, 0)

    @pl.when(turn_step < tiles)
    def _():
        at = pl.ds(pl.multiple_of(turn_step * tile, tile), tile)
        spec_ref[:, at, :] = spectra_tile(
            v_ref, h_ref, flag_ref, coeff_ref, table_ref, filtered_ref, wide_ref
        )

    @pl.when(turn_step == tiles)
    def _():
        stay = pltpu.make_async_copy(
            spec_ref.at[pl.ds(here * own, own)],
            x_ref.at[
                :,
                pl.ds(pl.multiple_of(c * inputs, inputs), inputs),
                pl.ds(pl.multiple_of(me * lanes, lanes), lanes),
            ],
            local.at[0],
        )
        stay.start()

        def finish(step, carry):
            spectra(step, True, 0, inputs).wait_send()
            spectra(step, False, 0, inputs).wait_recv()
            return carry

        def finish_weights(step, carry):
            weights(step, True).wait_send()
            weights(step, False).wait_recv()
            return carry

        lax.fori_loop(1, devices, finish, 0)
        lax.fori_loop(1, qs, finish_weights, 0)
        stay.wait()
        keep.wait()


def turn(voltages, input_flags, channel_order, beam_weights):
    cs, rs, qs = sizes()
    devices = cs * rs * qs
    own = NCH // devices
    _, inputs, samples = voltages.shape
    past = (TAPS - 1) * NCH
    history = passed_along(voltages[:, :, samples - past :], ("row", "col"), 1)
    frames = samples // NCH
    lanes = 2 * frames
    tile = 16
    group = 2 * tile if inputs % (2 * tile) == 0 else tile
    last = inputs // tile - 1
    tables = dft_tables(channel_order, NCH)[:, 0].reshape(NCH, 2 * NCH)
    anywhere = pl.BlockSpec(memory_space=pl.ANY)
    return pl.pallas_call(
        functools.partial(turn_kernel, cs, rs, qs, tile, group),
        grid=(inputs // tile + 1,),
        out_shape=(
            jax.ShapeDtypeStruct((own, inputs * cs, lanes * rs * qs), jnp.bfloat16),
            jax.ShapeDtypeStruct(
                (2, own, beam_weights.shape[2] * qs, beam_weights.shape[3]), beam_weights.dtype
            ),
        ),
        in_specs=[
            pl.BlockSpec((2, tile, samples), lambda i: (0, jnp.minimum(i, last), 0)),
            pl.BlockSpec((2, tile, past), lambda i: (0, jnp.minimum(i, last), 0)),
            pl.BlockSpec((tile, 1), lambda i: (jnp.minimum(i, last), 0)),
            pl.BlockSpec((TAPS, NCH), lambda i: (0, 0)),
            pl.BlockSpec((NCH, 2 * NCH), lambda i: (0, 0)),
            anywhere,
        ],
        out_specs=(anywhere,) * 2,
        scratch_shapes=[
            pltpu.VMEM((2, frames, tile, NCH), jnp.float32),
            pltpu.VMEM((NCH, tile, lanes), jnp.float32),
            pltpu.VMEM((NCH, inputs, lanes), jnp.bfloat16),
            pltpu.SemaphoreType.DMA((devices,)),
            pltpu.SemaphoreType.DMA((devices,)),
            pltpu.SemaphoreType.DMA((qs,)),
            pltpu.SemaphoreType.DMA((qs,)),
            pltpu.SemaphoreType.DMA((2,)),
        ],
        compiler_params=pltpu.CompilerParams(has_side_effects=True, vmem_limit_bytes=60 << 20),
        name="turn",
    )(
        voltages,
        history,
        input_flags.astype(jnp.float32)[:, None],
        prototype(TAPS, NCH),
        tables,
        beam_weights,
    )


def mirrored(half, rs, source, row, col):
    upper = row // half == 1
    second = (upper & (row > col)) | (jnp.logical_not(upper) & (row < col))
    return second & (row // half == col // half) & (source // half != row // half)


def products_kernel(
    rs, qs, frame_count,
    x_ref, w_ref, swap_ref, pool_ref, block_ref, part_ref,
    y_ref, vis_ref, power_ref, send, recv, relay_send, psend, precv, local,
):
    c, r, q = (lax.axis_index(name) for name in ("chan", "row", "col"))
    cells = rs * qs
    half = rs // 2
    me = r * qs + q
    own, inputs = vis_ref.shape[1], vis_ref.shape[2]
    depth = x_ref.shape[2]
    height, width = block_ref.shape[2], block_ref.shape[3]
    part_height, part_width = part_ref.shape[1], part_ref.shape[2]
    channel = pl.program_id(0)

    def ahead(step, sign):
        row = (r + rs + sign * (step % rs)) % rs
        return row * qs + (q + qs + sign * (step // rs)) % qs

    def vis_at(planes, first, count, row, col):
        return vis_ref.at[
            pl.ds(0, planes),
            pl.ds(first, count),
            pl.ds(pl.multiple_of(row * height, height), height),
            pl.ds(pl.multiple_of(col * width, width), width),
        ]

    def power_at(row, col):
        return power_ref.at[
            pl.ds(pl.multiple_of(col * part_height, part_height), part_height),
            pl.ds(pl.multiple_of(row * part_width, part_width), part_width),
        ]

    def landing(planes, slot, first, count):
        return block_ref.at[pl.ds(0, planes), pl.ds(slot * own + first, count)]

    def outgoing(planes, cell, first, count):
        return pltpu.make_async_remote_copy(
            src_ref=vis_at(planes, first, count, cell // qs, cell % qs),
            dst_ref=landing(planes, me, first, count),
            send_sem=send.at[cell],
            recv_sem=recv.at[me * own + first],
            device_id=(c, cell // qs, cell % qs),
            device_id_type=MESH,
        )

    def incoming(planes, slot, at):
        return pltpu.make_async_remote_copy(
            src_ref=landing(planes, slot, at, 1),
            dst_ref=landing(planes, slot, at, 1),
            send_sem=send.at[slot],
            recv_sem=recv.at[slot * own + at],
            device_id=(c, slot // qs, slot % qs),
            device_id_type=MESH,
        )

    def relay(slot, first, count):
        return pltpu.make_async_remote_copy(
            src_ref=landing(2, slot, first, count),
            dst_ref=landing(2, slot, first, count),
            send_sem=relay_send.at[slot],
            recv_sem=recv.at[slot * own + first],
            device_id=(c, q, r),
            device_id_type=MESH,
        )

    def both(diagonal, sent, act):
        @pl.when(sent & diagonal)
        def _():
            act(1)

        @pl.when(sent & jnp.logical_not(diagonal))
        def _():
            act(2)

    def part(step, leaving):
        cell = ahead(step, 1 if leaving else -1)
        slot = me if leaving else cell
        return pltpu.make_async_remote_copy(
            src_ref=power_at(cell // qs, cell % qs),
            dst_ref=part_ref.at[slot],
            send_sem=psend.at[cell],
            recv_sem=precv.at[slot],
            device_id=(c, cell // qs, cell % qs),
            device_id_type=MESH,
        )

    @pl.when(channel == 0)
    def _():
        power_ref[...] = jnp.zeros_like(power_ref)

    @pl.when(channel < own)
    def _():
        lanes = swap_ref.shape[0]
        across = (((1,), (1,)), ((), ()))

        def rows(step, carry):
            outward = jnp.where(step < half, half + step, rs - 1 - step)
            row = jnp.where(r < half, outward, rs - 1 - outward)
            at = pl.ds(pl.multiple_of(row * height, height), height)
            for start in range(0, depth, lanes):
                y_ref[at, start : start + lanes] = jnp.dot(
                    x_ref[0, at, start : start + lanes],
                    swap_ref[...],
                    preferred_element_type=jnp.float32,
                ).astype(jnp.bfloat16)
            re = lax.dot_general(
                x_ref[0, at, :], x_ref[0], across, preferred_element_type=jnp.float32
            )
            im = lax.dot_general(y_ref[at, :], x_ref[0], across, preferred_element_type=jnp.float32)
            panel = lax.broadcasted_iota(jnp.int32, re.shape, 1) // width
            first = jnp.where(panel == row, re + im, re)
            vis_ref[0, channel, at, :] = (first / frame_count).astype(vis_ref.dtype)
            vis_ref[1, channel, at, :] = (im / frame_count).astype(vis_ref.dtype)

            def start(step, carry):
                col = (q + step) % qs
                cell = row * qs + col
                sent = (cell != me) & jnp.logical_not(mirrored(half, rs, r, row, col))
                both(row == col, sent, lambda planes: outgoing(planes, cell, channel, 1).start())
                return carry

            lax.fori_loop(0, qs, start, 0)
            return carry

        lax.fori_loop(0, rs, rows, 0)
        span = 4 * lanes if depth % (4 * lanes) == 0 else lanes

        def columns(step, carry):
            at = pl.ds(pl.multiple_of(step * span, span), span)
            beam = jnp.dot(w_ref[0, 0], x_ref[0, :, at], preferred_element_type=jnp.float32)
            beam = beam - jnp.dot(w_ref[1, 0], y_ref[:, at], preferred_element_type=jnp.float32)
            square = beam * beam
            high = square.astype(jnp.bfloat16)
            low = (square - high.astype(jnp.float32)).astype(jnp.bfloat16)
            pool = pool_ref[at, :]
            return (
                carry
                + jnp.dot(high, pool, preferred_element_type=jnp.float32)
                + jnp.dot(low, pool, preferred_element_type=jnp.float32)
            )

        found = lax.fori_loop(0, depth // span, columns, jnp.zeros(power_ref.shape, jnp.float32))
        lane = lax.broadcasted_iota(jnp.int32, power_ref.shape, 1) % part_width
        power_ref[...] = jnp.where(lane // (part_width // own) == channel, found, power_ref[...])

    @pl.when(channel == own)
    def _():
        stay = pltpu.make_async_copy(vis_at(2, 0, own, r, q), landing(2, me, 0, own), local.at[0])
        keep = pltpu.make_async_copy(power_at(r, q), part_ref.at[me], local.at[1])

        def start(step, carry):
            part(step, True).start()
            return carry

        lax.fori_loop(1, cells, start, 0)
        stay.start()
        keep.start()
        upper = r // half == 1
        relays = (r // half == q // half) & (
            (upper & (r < q)) | (jnp.logical_not(upper) & (r > q))
        )
        far = (1 - r // half) * half * qs

        @pl.when(relays)
        def _():
            def pass_on(step, carry):
                slot, at = far + step % (half * qs), step // (half * qs)
                incoming(2, slot, at).wait_recv()
                relay(slot, at, 1).start()
                return carry

            lax.fori_loop(0, half * qs * own, pass_on, 0)

        def finish(step, carry):
            cell = ahead(step, 1)
            row, col = cell // qs, cell % qs
            sent = jnp.logical_not(mirrored(half, rs, r, row, col))
            both(row == col, sent, lambda planes: outgoing(planes, cell, 0, own).wait_send())
            slot = ahead(step, -1)
            passed = relays & (slot // qs // half != r // half)

            def arrive(planes):
                for at in range(own):
                    incoming(planes, slot, at).wait_recv()

            both(r == q, jnp.logical_not(passed), arrive)
            part(step, True).wait_send()
            part(step, False).wait_recv()
            return carry

        lax.fori_loop(1, cells, finish, 0)

        @pl.when(relays)
        def _():
            def passed_on(step, carry):
                relay(far + step, 0, own).wait_send()
                return carry

            lax.fori_loop(0, half * qs, passed_on, 0)

        stay.wait()
        keep.wait()


def unpack_kernel(rs, qs, block_ref, eye_ref, out_ref):
    r, q = (lax.axis_index(name) for name in ("row", "col"))
    source = pl.program_id(0) // qs
    turned = mirrored(rs // 2, rs, source, r, q)

    def turn_over(value):
        return lax.dot_general(
            eye_ref[...], value, (((1,), (1,)), ((), ())), preferred_element_type=jnp.float32
        )

    @pl.when(r == q)
    def _():
        for at in range(out_ref.shape[1]):
            packed = block_ref[0, at]
            wide, over = packed.astype(jnp.float32), turn_over(packed)
            out_ref[0, at] = 0.5 * (wide + over)
            out_ref[1, at] = 0.5 * (wide - over)

    @pl.when(turned)
    def _():
        for at in range(out_ref.shape[1]):
            out_ref[0, at] = turn_over(block_ref[0, at])
            out_ref[1, at] = -turn_over(block_ref[1, at])

    @pl.when((r != q) & jnp.logical_not(turned))
    def _():
        out_ref[...] = block_ref[...].astype(jnp.float32)


def unpack(block, own):
    _, rs, qs = sizes()
    _, channels, height, width = block.shape
    return pl.pallas_call(
        functools.partial(unpack_kernel, rs, qs),
        grid=(channels // own,),
        out_shape=jax.ShapeDtypeStruct(block.shape, jnp.float32),
        in_specs=[
            pl.BlockSpec((2, own, height, width), lambda i: (0, i, 0, 0)),
            pl.BlockSpec((height, width), lambda i: (0, 0)),
        ],
        out_specs=pl.BlockSpec((2, own, height, width), lambda i: (0, i, 0, 0)),
        compiler_params=pltpu.CompilerParams(vmem_limit_bytes=40 << 20),
        name="unpack",
    )(block, jnp.eye(height, dtype=jnp.bfloat16))


def products(x, weights, frames):
    _, rs, qs = sizes()
    cells = rs * qs
    own, inputs, depth = x.shape
    beams = weights.shape[2]
    bins = depth // (2 * INTEG)
    lanes = 2 * frames
    last = own - 1
    source = jnp.arange(lanes)[:, None]
    goal = jnp.arange(lanes)[None, :]
    swap = jnp.where(source == goal + frames, 1.0, 0.0) - jnp.where(source + frames == goal, 1.0, 0.0)
    at = jnp.arange(depth)
    frame = at // lanes * frames + at % frames
    part = bins // rs
    column = jnp.arange(rs * own * part)
    bin_of = column // (own * part) * part + column % part
    pool = jnp.where(frame[:, None] // INTEG == bin_of[None, :], 1.0 / INTEG, 0.0)
    anywhere = pl.BlockSpec(memory_space=pl.ANY)
    return pl.pallas_call(
        functools.partial(products_kernel, rs, qs, depth // 2),
        grid=(own + 1,),
        out_shape=(
            jax.ShapeDtypeStruct((2, cells * own, inputs // rs, inputs // qs), jnp.bfloat16),
            jax.ShapeDtypeStruct((cells, beams // qs, own * part), jnp.float32),
        ),
        in_specs=[
            pl.BlockSpec((1, inputs, depth), lambda j: (jnp.minimum(j, last), 0, 0)),
            pl.BlockSpec((2, 1, beams, inputs), lambda j: (0, jnp.minimum(j, last), 0, 0)),
            pl.BlockSpec((lanes, lanes), lambda j: (0, 0)),
            pl.BlockSpec((depth, rs * own * part), lambda j: (0, 0)),
        ],
        out_specs=(anywhere,) * 2,
        scratch_shapes=[
            pltpu.VMEM((inputs, depth), jnp.bfloat16),
            pltpu.VMEM((2, own, inputs, inputs), jnp.bfloat16),
            pltpu.VMEM((beams, rs * own * part), jnp.float32),
        ]
        + [pltpu.SemaphoreType.DMA((count,)) for count in (cells, cells * own)]
        + [pltpu.SemaphoreType.DMA((cells,))] * 3
        + [pltpu.SemaphoreType.DMA((2,))],
        compiler_params=pltpu.CompilerParams(has_side_effects=True, vmem_limit_bytes=60 << 20),
        name="products",
    )(x, weights, swap.astype(jnp.bfloat16), pool.astype(jnp.bfloat16))


def by_channels(voltages, input_flags, channel_order, beam_weights):
    x, weights = turn(voltages, input_flags, channel_order, beam_weights)
    block, part = products(x, weights, voltages.shape[2] // NCH)
    own = x.shape[0]
    cells, beams, _ = part.shape
    split = part.reshape(cells, beams, own, -1)
    beam_power = jnp.transpose(split, (0, 2, 1, 3)).reshape(cells * own, beams, -1)
    return (unpack(block, own), beam_power)


def on_device(voltages, input_flags, channel_order, beam_weights):
    cs, rs, qs = sizes()
    lanes = 2 * (voltages.shape[2] // NCH)
    devices = cs * rs * qs
    square = rs == qs and rs % 2 == 0
    whole = square and NCH % devices == 0 and lanes % 128 == 0 and voltages.shape[1] % 16 == 0
    if whole and NCH // devices * (lanes // 2 * qs // INTEG) % 128 == 0:
        plan = by_channels
    else:
        plan = by_panels
    return plan(voltages, input_flags, channel_order, beam_weights)


def solution(mesh):
    placed = (P(None, "chan", ("row", "col")), P("chan"), P(), P(None, "chan", "col", None))
    return jax.shard_map(
        on_device,
        mesh=mesh,
        in_specs=placed,
        out_specs=(P(None, "chan", "row", "col"), P("chan", "col", "row")),
        check_vma=False,
    )
```

```python
import functools
import math

import jax
import jax.numpy as jnp
import numpy as np
from jax import lax
from jax.experimental import pallas as pl
from jax.experimental.pallas import tpu as pltpu
from jax.sharding import PartitionSpec as P

NCH = 128
TAPS = 4
INTEG = 8


def passed_along(value, axis, steps):
    count = lax.axis_size(axis)
    initial, last = (max(0, -steps), min(count, count - steps))
    return lax.ppermute(value, axis, [(source, source + steps) for source in range(initial, last)])


def prototype(taps, length):
    position = jnp.arange(taps * length, dtype=jnp.float32) + 0.5
    offset = position / length - taps / 2.0
    window = 0.5 - 0.5 * jnp.cos(2.0 * math.pi * position / (taps * length))
    return (jnp.sin(math.pi * offset) / (math.pi * offset) * window).reshape(taps, length)


def dft_tables(channel_rows, length):
    sample_index = jnp.arange(length, dtype=jnp.int32)
    product = channel_rows[:, None] * sample_index[None, :] % length
    angle = 2.0 * math.pi / length * product.astype(jnp.float32)
    factor = 1.0 / math.sqrt(length)
    cosine = jnp.cos(angle) * factor
    sine = jnp.sin(angle) * factor
    real_rows = jnp.stack([cosine, sine], axis=1)
    imag_rows = jnp.stack([-sine, cosine], axis=1)
    return jnp.stack([real_rows, imag_rows], axis=1).astype(jnp.bfloat16)


def to_frames(gathered, frames, outer, inner, swapped):
    chans = gathered.shape[0]
    width = gathered.shape[1]
    split = gathered.reshape(chans, width, outer, inner, 2, frames)
    if swapped:
        order = jnp.transpose(split, (0, 4, 1, 3, 2, 5))
    else:
        order = jnp.transpose(split, (0, 4, 1, 2, 3, 5))
    return order.reshape(chans, 2, width, outer * inner * frames)


def correlate_one(left_block, right_block, frame_count):
    left_re = left_block[0]
    left_im = left_block[1]
    right_re = right_block[0]
    right_im = right_block[1]
    dims = (((1,), (1,)), ((), ()))
    vis_re = lax.dot_general(left_re, right_re, dims, preferred_element_type=jnp.float32)
    vis_re = vis_re + lax.dot_general(left_im, right_im, dims, preferred_element_type=jnp.float32)
    vis_im = lax.dot_general(left_im, right_re, dims, preferred_element_type=jnp.float32)
    vis_im = vis_im - lax.dot_general(left_re, right_im, dims, preferred_element_type=jnp.float32)
    return jnp.stack([vis_re, vis_im]) / frame_count


def correlate(left_view, right_view, frame_count):
    result = lax.map(
        lambda items: correlate_one(items[0], items[1], frame_count), (left_view, right_view)
    )
    return jnp.transpose(result, (1, 0, 2, 3))


def beams_one(weights, block):
    w_real = weights[0]
    w_imag = weights[1]
    x_real = block[0]
    x_imag = block[1]
    beam_re = jnp.dot(w_real, x_real, preferred_element_type=jnp.float32) - jnp.dot(
        w_imag, x_imag, preferred_element_type=jnp.float32
    )
    beam_im = jnp.dot(w_real, x_imag, preferred_element_type=jnp.float32) + jnp.dot(
        w_imag, x_real, preferred_element_type=jnp.float32
    )
    return jnp.stack([beam_re, beam_im], axis=1)


def form_beams(weights, view):
    by_channel = jnp.transpose(weights, (1, 0, 2, 3))
    return lax.map(lambda items: beams_one(items[0], items[1]), (by_channel, view))


def integrate(voltage):
    power = voltage[:, :, 0] * voltage[:, :, 0] + voltage[:, :, 1] * voltage[:, :, 1]
    return power.reshape(power.shape[0], power.shape[1], -1, INTEG).mean(axis=-1)


def channelize(voltages, input_flags, channel_order):
    masked = voltages * input_flags.astype(jnp.bfloat16)[None, :, None]
    local_inputs = masked.shape[1]
    frames = masked.shape[2] // NCH
    history = passed_along(masked[:, :, masked.shape[2] - (TAPS - 1) * NCH :], ("row", "col"), 1)
    joined = jnp.concatenate([history, masked], axis=2)
    blocks = joined.reshape(2, local_inputs, frames + TAPS - 1, NCH)
    coeffs = prototype(TAPS, NCH)
    filtered = jnp.zeros((2, local_inputs, frames, NCH), jnp.float32)
    for tap_index in range(TAPS):
        filtered = filtered + coeffs[tap_index] * blocks[
            :, :, tap_index : tap_index + frames
        ].astype(jnp.float32)
    filtered = filtered.astype(jnp.bfloat16)
    tables = dft_tables(channel_order, NCH)
    spectrum = jnp.einsum(
        "kqpn,pifn->kiqf",
        tables.astype(jnp.float32),
        filtered.astype(jnp.float32),
        precision=lax.Precision.HIGHEST,
    ).astype(jnp.bfloat16)
    spectrum = spectrum.reshape(NCH, local_inputs, 2 * frames)
    return spectrum


def by_panels(voltages, input_flags, channel_order, beam_weights):
    spectrum = channelize(voltages, input_flags, channel_order)
    frames = spectrum.shape[2] // 2
    turned = lax.all_to_all(spectrum, "chan", split_axis=0, concat_axis=1, tiled=True)
    row_count = lax.axis_size("row")
    col_count = lax.axis_size("col")
    total_frames = frames * row_count * col_count
    row_turned = lax.all_to_all(turned, "row", split_axis=1, concat_axis=2, tiled=True)
    row_all = lax.all_gather(row_turned, "col", axis=2, tiled=True)
    col_turned = lax.all_to_all(turned, "col", split_axis=1, concat_axis=2, tiled=True)
    col_all = lax.all_gather(col_turned, "row", axis=2, tiled=True)
    row_view = to_frames(row_all, frames, col_count, row_count, True)
    col_view = to_frames(col_all, frames, row_count, col_count, False)
    visibility = correlate(row_view, col_view, total_frames)
    weights_all = lax.all_gather(beam_weights, "col", axis=2, tiled=True)
    local_view = to_frames(turned, frames, 1, 1, False)
    voltage = form_beams(weights_all, local_view)
    own_power = integrate(voltage)
    beam_power = lax.all_to_all(own_power, "col", split_axis=1, concat_axis=2, tiled=True)
    return (visibility, beam_power)


MESH = pl.DeviceIdType.MESH


def spectra_tile(v_ref, h_ref, flag_ref, coeff_ref, table_ref, filtered_ref, wide_ref):
    tile = v_ref.shape[1]
    frames = v_ref.shape[2] // NCH
    lanes = 2 * frames
    flag = jnp.broadcast_to(flag_ref[...], (tile, NCH))
    rows = [jnp.broadcast_to(coeff_ref[tap : tap + 1, :], (tile, NCH)) for tap in range(TAPS)]
    for part in range(2):

        def frame_at(index):
            ref, at = (h_ref, index) if index < TAPS - 1 else (v_ref, index - TAPS + 1)
            return ref[part, :, at * NCH : (at + 1) * NCH].astype(jnp.float32) * flag

        window = [frame_at(index) for index in range(TAPS - 1)]
        for frame in range(frames):
            window = window[-(TAPS - 1) :] + [frame_at(frame + TAPS - 1)]
            total = rows[0] * window[0]
            for tap in range(1, TAPS):
                total = total + rows[tap] * window[tap]
            filtered_ref[part, frame] = total
    for first in range(0, tile, 2):
        stack = []
        for index in (first, first + 1):
            re = filtered_ref[0, :, index, :].astype(jnp.bfloat16)
            im = filtered_ref[1, :, index, :].astype(jnp.bfloat16)
            stack.append(jnp.concatenate([re, im], axis=1))
            stack.append(jnp.concatenate([im, -re], axis=1))
        both = lax.dot_general(
            table_ref[...],
            jnp.concatenate(stack, axis=0),
            (((1,), (1,)), ((), ())),
            preferred_element_type=jnp.float32,
        )
        wide_ref[:, first, :] = both[:, :lanes]
        wide_ref[:, first + 1, :] = both[:, lanes:]
    return wide_ref[...].astype(jnp.bfloat16)


def sizes():
    return lax.axis_size("chan"), lax.axis_size("row"), lax.axis_size("col")


def part_of(c, r, q, cs, half, qs, step, sign):
    chan = (c + cs + sign * (step % cs)) % cs
    inner = step // cs
    row = r // half * half + (r % half + half + sign * (inner % half)) % half
    return chan, row, (q + qs + sign * (inner // half)) % qs


def turn_kernel(
    cs, rs, qs, tile, group, wide, alone, early,
    v_ref, h_ref, flag_ref, coeff_ref, table_ref, x_ref, e_ref, s_ref,
    filtered_ref, wide_ref, spec_ref, send, recv, esend, erecv, local,
):
    c, r, q = (lax.axis_index(name) for name in ("chan", "row", "col"))
    half = rs // 2
    cells = rs * qs
    halves = half * qs
    devices = cs * cells
    me = r * qs + q
    mine = me % halves
    here = c * cells + me
    inputs = spec_ref.shape[1]
    lanes = spec_ref.shape[2]
    early_base = devices * alone
    late_base = early_base + cs * halves * early
    turn_step = pl.program_id(0)
    tiles = inputs // tile

    def ahead(step, sign):
        row = (r + rs + sign * (step % rs)) % rs
        return row * qs + (q + qs + sign * (step // rs)) % qs

    def rows_at(first, count):
        return pl.ds(pl.multiple_of(first, tile), count)

    def spectra(step, outgoing, first, count):
        if outgoing:
            chan, cell = (c + step % cs) % cs, ahead(step // cs, 1)
            origin, column = c, me
            slot = here
        else:
            chan, cell = (c + cs - step % cs) % cs, ahead(step // cs, -1)
            origin, column = chan, cell
            slot = chan * cells + cell
        return pltpu.make_async_remote_copy(
            src_ref=spec_ref.at[
                pl.ds((chan * cells + cell) * alone, alone), rows_at(first, count)
            ],
            dst_ref=x_ref.at[
                :,
                rows_at(origin * inputs + first, count),
                pl.ds(pl.multiple_of(column * lanes, lanes), lanes),
            ],
            send_sem=send.at[chan * cells + cell],
            recv_sem=recv.at[slot],
            device_id=(chan, cell // qs, cell % qs),
            device_id_type=MESH,
        )

    def sooner(step, outgoing, first, count):
        chan, row, col = part_of(c, r, q, cs, half, qs, step, 1 if outgoing else -1)
        place = row % half * qs + col
        origin, column = (c, mine) if outgoing else (chan, place)
        return pltpu.make_async_remote_copy(
            src_ref=spec_ref.at[
                pl.ds(early_base + (chan * halves + place) * early, early), rows_at(first, count)
            ],
            dst_ref=e_ref.at[
                :,
                rows_at(origin * inputs + first, count),
                pl.ds(pl.multiple_of(column * lanes, lanes), lanes),
            ],
            send_sem=esend.at[chan * halves + place],
            recv_sem=erecv.at[origin * halves + column],
            device_id=(chan, row, col),
            device_id_type=MESH,
        )

    @pl.when((turn_step > 0) & (turn_step * tile % group == 0))
    def _():
        def start(step, carry):
            spectra(step, True, turn_step * tile - group, group).start()
            return carry

        lax.fori_loop(1, devices, start, 0)

    @pl.when((turn_step > 0) & (turn_step * tile % wide == 0))
    def _():
        def start(step, carry):
            sooner(step, True, turn_step * tile - wide, wide).start()
            return carry

        lax.fori_loop(1, cs * halves, start, 0)

    @pl.when(turn_step < tiles)
    def _():
        at = pl.ds(pl.multiple_of(turn_step * tile, tile), tile)
        spec_ref[:, at, :] = spectra_tile(
            v_ref, h_ref, flag_ref, coeff_ref, table_ref, filtered_ref, wide_ref
        )

    @pl.when(turn_step == tiles)
    def _():
        stays = [
            pltpu.make_async_copy(
                spec_ref.at[pl.ds(here * alone, alone)],
                x_ref.at[
                    :, rows_at(c * inputs, inputs), pl.ds(pl.multiple_of(me * lanes, lanes), lanes)
                ],
                local.at[0],
            ),
            pltpu.make_async_copy(
                spec_ref.at[pl.ds(early_base + (c * halves + mine) * early, early)],
                e_ref.at[
                    :,
                    rows_at(c * inputs, inputs),
                    pl.ds(pl.multiple_of(mine * lanes, lanes), lanes),
                ],
                local.at[1],
            ),
            pltpu.make_async_copy(
                spec_ref.at[pl.ds(late_base, s_ref.shape[0])], s_ref, local.at[2]
            ),
        ]
        for stay in stays:
            stay.start()

        def finish(step, carry):
            spectra(step, True, 0, inputs).wait_send()
            spectra(step, False, 0, inputs).wait_recv()
            return carry

        def finish_sooner(step, carry):
            sooner(step, True, 0, inputs).wait_send()
            sooner(step, False, 0, inputs).wait_recv()
            return carry

        lax.fori_loop(1, devices, finish, 0)
        lax.fori_loop(1, cs * halves, finish_sooner, 0)
        for stay in stays:
            stay.wait()


def turn(voltages, input_flags, channel_order, alone, shared, early):
    cs, rs, qs = sizes()
    devices = cs * rs * qs
    halves = rs // 2 * qs
    _, inputs, samples = voltages.shape
    past = (TAPS - 1) * NCH
    history = passed_along(voltages[:, :, samples - past :], ("row", "col"), 1)
    frames = samples // NCH
    lanes = 2 * frames
    tile = 16
    group = 2 * tile if inputs % (2 * tile) == 0 else tile
    wide = 4 * group if inputs % (4 * group) == 0 else group
    last = inputs // tile - 1
    place = jnp.arange(NCH).reshape(cs, NCH // cs)
    split = place[:, rs * qs * alone :].reshape(cs, halves, shared)
    order = jnp.concatenate(
        [
            place[:, : rs * qs * alone].reshape(-1),
            split[:, :, :early].reshape(-1),
            split[:, :, early:].reshape(-1),
        ]
    )
    tables = dft_tables(channel_order[order], NCH)[:, 0].reshape(NCH, 2 * NCH)
    anywhere = pl.BlockSpec(memory_space=pl.ANY)
    counts = (devices, devices, cs * halves, cs * halves, 3)
    return pl.pallas_call(
        functools.partial(turn_kernel, cs, rs, qs, tile, group, wide, alone, early),
        grid=(inputs // tile + 1,),
        out_shape=(
            jax.ShapeDtypeStruct((alone, inputs * cs, lanes * rs * qs), jnp.bfloat16),
            jax.ShapeDtypeStruct((early, inputs * cs, lanes * halves), jnp.bfloat16),
            jax.ShapeDtypeStruct((cs * halves * (shared - early), inputs, lanes), jnp.bfloat16),
        ),
        in_specs=[
            pl.BlockSpec((2, tile, samples), lambda i: (0, jnp.minimum(i, last), 0)),
            pl.BlockSpec((2, tile, past), lambda i: (0, jnp.minimum(i, last), 0)),
            pl.BlockSpec((tile, 1), lambda i: (jnp.minimum(i, last), 0)),
            pl.BlockSpec((TAPS, NCH), lambda i: (0, 0)),
            pl.BlockSpec((NCH, 2 * NCH), lambda i: (0, 0)),
        ],
        out_specs=(anywhere,) * 3,
        scratch_shapes=[
            pltpu.VMEM((2, frames, tile, NCH), jnp.float32),
            pltpu.VMEM((NCH, tile, lanes), jnp.float32),
            pltpu.VMEM((NCH, inputs, lanes), jnp.bfloat16),
        ]
        + [pltpu.SemaphoreType.DMA((count,)) for count in counts],
        compiler_params=pltpu.CompilerParams(has_side_effects=True, vmem_limit_bytes=60 << 20),
        name="turn",
    )(
        voltages,
        history,
        input_flags.astype(jnp.float32)[:, None],
        prototype(TAPS, NCH),
        tables,
    )


def direct_pair(half, source_row, source_col, row, col, shared):
    upper = row // half == 1
    crossing = (row != col) & (row // half == col // half) & (source_row // half != row // half)
    nearer = (upper & (row < col)) | (jnp.logical_not(upper) & (row > col))
    if shared:
        other = source_col // half != row // half
        nearer = (nearer & jnp.logical_not(other)) | (jnp.logical_not(nearer) & other)
    return crossing, nearer


def relayed(*args):
    crossing, direct = direct_pair(*args)
    return crossing & direct


def mirrored(*args):
    crossing, direct = direct_pair(*args)
    return crossing & jnp.logical_not(direct)


def products_kernel(
    cs, rs, qs, frame_count, alone, early,
    xa_ref, xe_ref, s_ref, weight_ref, swap_ref, pool_ref,
    block_ref, parta_ref, partb_ref, late_ref, all_ref,
    x_ref, y_ref, w_ref, vis_ref, powera_ref, powerb_ref,
    load, senda, sendb, recv, relaya, relayb,
    psenda, precva, psendb, precvb, lsend, lrecv, wsend, wrecv, wload, local,
):
    c, r, q = (lax.axis_index(name) for name in ("chan", "row", "col"))
    cells = rs * qs
    half = rs // 2
    halves = half * qs
    me = r * qs + q
    mine = me % halves
    held, inputs = vis_ref.shape[1], vis_ref.shape[2]
    shared = held - alone
    late = shared - early
    depth = x_ref.shape[2]
    depths = {False: depth, True: depth // 2}
    lanes = swap_ref.shape[0]
    own_inputs = inputs // cs
    height, width = block_ref.shape[2], block_ref.shape[3]
    part_height, part_width = parta_ref.shape[1], parta_ref.shape[2]
    now = pl.program_id(0)

    def ahead(step, sign):
        row = (r + rs + sign * (step % rs)) % rs
        return row * qs + (q + qs + sign * (step // rs)) % qs

    def vis_at(planes, first, count, row, col):
        return vis_ref.at[
            pl.ds(0, planes),
            pl.ds(first, count),
            pl.ds(pl.multiple_of(row * height, height), height),
            pl.ds(pl.multiple_of(col * width, width), width),
        ]

    def power_at(ref, row, col):
        return ref.at[
            pl.ds(pl.multiple_of(col * part_height, part_height), part_height),
            pl.ds(pl.multiple_of(row * part_width, part_width), part_width),
        ]

    def landing(kind, planes, cell, first, count):
        base = cells * alone + cell * shared if kind else cell * alone
        return block_ref.at[pl.ds(0, planes), pl.ds(base + first, count)]

    def arrival(kind, cell, first):
        return recv.at[cell * held + first + (alone if kind else 0)]

    def outgoing(kind, planes, cell, first, count):
        return pltpu.make_async_remote_copy(
            src_ref=vis_at(planes, first + (alone if kind else 0), count, cell // qs, cell % qs),
            dst_ref=landing(kind, planes, me, first, count),
            send_sem=(sendb if kind else senda).at[cell],
            recv_sem=arrival(kind, me, first),
            device_id=(c, cell // qs, cell % qs),
            device_id_type=MESH,
        )

    def incoming(kind, planes, slot, at):
        return pltpu.make_async_remote_copy(
            src_ref=landing(kind, planes, slot, at, 1),
            dst_ref=landing(kind, planes, slot, at, 1),
            send_sem=senda.at[slot],
            recv_sem=arrival(kind, slot, at),
            device_id=(c, slot // qs, slot % qs),
            device_id_type=MESH,
        )

    def relay(kind, slot, first, count):
        return pltpu.make_async_remote_copy(
            src_ref=landing(kind, 2, slot, first, count),
            dst_ref=landing(kind, 2, slot, first, count),
            send_sem=(relayb if kind else relaya).at[slot],
            recv_sem=arrival(kind, slot, first),
            device_id=(c, q, r),
            device_id_type=MESH,
        )

    def both(diagonal, sent, act):
        @pl.when(sent & diagonal)
        def _():
            act(1)

        @pl.when(sent & jnp.logical_not(diagonal))
        def _():
            act(2)

    def part(kind, cell, slot):
        source, goal = (powerb_ref, partb_ref) if kind else (powera_ref, parta_ref)
        leaves, comes = (psendb, precvb) if kind else (psenda, precva)
        row = cell // qs % half if kind else cell // qs
        place = slot % halves if kind else slot
        return pltpu.make_async_remote_copy(
            src_ref=power_at(source, row, cell % qs),
            dst_ref=goal.at[place],
            send_sem=leaves.at[cell],
            recv_sem=comes.at[slot],
            device_id=(c, cell // qs, cell % qs),
            device_id_type=MESH,
        )

    def spread(step, leaving, at):
        chan, row, col = part_of(c, r, q, cs, half, qs, step, 1 if leaving else -1)
        place = row % half * qs + col
        origin, column = (c, mine) if leaving else (chan, place)
        peers = cs * halves
        return pltpu.make_async_remote_copy(
            src_ref=s_ref.at[(chan * halves + place) * late + at],
            dst_ref=late_ref.at[
                at,
                pl.ds(pl.multiple_of(origin * own_inputs, own_inputs), own_inputs),
                pl.ds(pl.multiple_of(column * lanes, lanes), lanes),
            ],
            send_sem=lsend.at[at * peers + chan * halves + place],
            recv_sem=lrecv.at[at * peers + origin * halves + column],
            device_id=(chan, row, col),
            device_id_type=MESH,
        )

    def stay_late(at):
        return pltpu.make_async_copy(
            s_ref.at[(c * halves + mine) * late + at],
            late_ref.at[
                at,
                pl.ds(pl.multiple_of(c * own_inputs, own_inputs), own_inputs),
                pl.ds(pl.multiple_of(mine * lanes, lanes), lanes),
            ],
            local.at[4],
        )

    def fetch(source, slot, kind):
        return pltpu.make_async_copy(
            source, x_ref.at[slot, :, pl.ds(0, depths[kind])], load.at[slot]
        )

    def weight_spans(peer):
        cell = r * qs + peer
        return (
            (cell * alone, 0, alone),
            (cells * alone + cell % halves * shared, alone, shared),
        )

    def weights_at(slot, goal, count):
        beams = weight_ref.shape[2]
        return all_ref.at[
            :, pl.ds(goal, count), pl.ds(pl.multiple_of(slot * beams, beams), beams)
        ]

    def weights(peer, slot, source, goal, count):
        return pltpu.make_async_remote_copy(
            src_ref=weight_ref.at[:, pl.ds(source, count)],
            dst_ref=weights_at(slot, goal, count),
            send_sem=wsend.at[peer],
            recv_sem=wrecv.at[slot],
            device_id=(c, r, peer),
            device_id_type=MESH,
        )

    keeps = [
        pltpu.make_async_copy(
            weight_ref.at[:, pl.ds(source, count)], weights_at(q, goal, count), local.at[5 + index]
        )
        for index, (source, goal, count) in enumerate(weight_spans(q))
    ]

    def fetch_weights(index, slot):
        return pltpu.make_async_copy(all_ref.at[:, index], w_ref.at[slot], wload.at[slot])

    def visibility_of(kind, slot, at):
        deep = depths[kind]
        across = (((1,), (1,)), ((), ()))
        index = at + (alone if kind else 0)

        def panels(step, carry):
            col = (q + step) % qs
            span = pl.ds(pl.multiple_of(col * width, width), width)
            for start in range(0, deep, lanes):
                y_ref[:, start : start + lanes] = jnp.dot(
                    x_ref[slot, span, start : start + lanes],
                    swap_ref[...],
                    preferred_element_type=jnp.float32,
                ).astype(jnp.bfloat16)
            every = x_ref[slot, :, :deep]
            re = lax.dot_general(
                every, x_ref[slot, span, :deep], across, preferred_element_type=jnp.float32
            )
            im = lax.dot_general(every, y_ref[:, :deep], across, preferred_element_type=jnp.float32)
            panel = lax.broadcasted_iota(jnp.int32, re.shape, 0) // height
            first = jnp.where(panel == col, re + im, re)
            vis_ref[0, index, :, span] = (first / frame_count).astype(vis_ref.dtype)
            vis_ref[1, index, :, span] = (im / frame_count).astype(vis_ref.dtype)

            def start(step, carry):
                outward = jnp.where(step % 2 == 0, half + step // 2, half - 1 - step // 2)
                row = jnp.where(r < half, outward, rs - 1 - outward)
                cell = row * qs + col
                sent = (cell != me) & jnp.logical_not(mirrored(half, r, q, row, col, kind))
                both(row == col, sent, lambda planes: outgoing(kind, planes, cell, at, 1).start())
                return carry

            lax.fori_loop(0, rs, start, 0)
            return carry

        lax.fori_loop(0, qs, panels, 0)

    def beams_of(kind, slot, at):
        deep = depths[kind]
        span = 4 * lanes if deep % (4 * lanes) == 0 else lanes
        power_ref = powerb_ref if kind else powera_ref
        columns_out = power_ref.shape[1]
        middle = lanes // 2

        def columns(step, carry):
            along = pl.ds(pl.multiple_of(step * span, span), span)
            x = x_ref[slot, :, along]
            straight = jnp.dot(w_ref[slot, 0], x, preferred_element_type=jnp.float32)
            crossed = jnp.dot(w_ref[slot, 1], x, preferred_element_type=jnp.float32)
            swapped = []
            for start in range(0, span, lanes):
                swapped.append(crossed[:, start + middle : start + lanes])
                swapped.append(-crossed[:, start : start + middle])
            beam = straight - jnp.concatenate(swapped, axis=1)
            square = beam * beam
            high = square.astype(jnp.bfloat16)
            low = (square - high.astype(jnp.float32)).astype(jnp.bfloat16)
            pool = pool_ref[along, :columns_out]
            return (
                carry
                + jnp.dot(high, pool, preferred_element_type=jnp.float32)
                + jnp.dot(low, pool, preferred_element_type=jnp.float32)
            )

        found = lax.fori_loop(0, deep // span, columns, jnp.zeros(power_ref.shape, jnp.float32))
        lane = lax.broadcasted_iota(jnp.int32, power_ref.shape, 1) % part_width
        power_ref[...] = jnp.where(lane // (part_width // shared) == at, found, power_ref[...])

    def pass_on(kind, at):
        far = (1 - r // half) * halves

        def one(step, carry):
            slot = far + step

            @pl.when(relayed(half, slot // qs, slot % qs, r, q, kind))
            def _():
                incoming(kind, 2, slot, at).wait_recv()
                relay(kind, slot, at, 1).start()

            return carry

        lax.fori_loop(0, halves, one, 0)

    locals_ = [
        pltpu.make_async_copy(
            vis_at(2, 0, alone, r, q), landing(False, 2, me, 0, alone), local.at[0]
        ),
        pltpu.make_async_copy(
            vis_at(2, alone, shared, r, q), landing(True, 2, me, 0, shared), local.at[1]
        ),
        pltpu.make_async_copy(power_at(powera_ref, r, q), parta_ref.at[me], local.at[2]),
        pltpu.make_async_copy(power_at(powerb_ref, r % half, q), partb_ref.at[mine], local.at[3]),
    ]
    coming = (now + 1) % held
    next_slot = (now + 1) % 2
    more = now + 1 < 2 * held
    turn_index = now % held

    @pl.when(now == 0)
    def _():
        powera_ref[...] = jnp.zeros_like(powera_ref)
        powerb_ref[...] = jnp.zeros_like(powerb_ref)
        fetch(xa_ref.at[0], 0, False).start()

    @pl.when(now < late)
    def _():
        def start(step, carry):
            spread(step, True, now).start()
            return carry

        lax.fori_loop(1, cs * halves, start, 0)
        stay = stay_late(now)
        stay.start()
        stay.wait()

    @pl.when(now == late)
    def _():
        def start(step, carry):
            peer = (q + step) % qs
            for source, goal, count in weight_spans(peer):
                weights(peer, q, source, goal, count).start()
            return carry

        lax.fori_loop(1, qs, start, 0)
        for keep in keeps:
            keep.start()

    @pl.when(more & (coming < alone))
    def _():
        fetch(xa_ref.at[coming], next_slot, False).start()

    @pl.when(more & (coming >= alone) & (coming < alone + early))
    def _():
        fetch(xe_ref.at[coming - alone], next_slot, True).start()

    @pl.when(now == held)
    def _():
        def arrive(step, carry):
            behind = (q + qs - step) % qs
            weights(behind, behind, 0, 0, held).wait_recv()
            return carry

        lax.fori_loop(1, qs, arrive, 0)
        for keep in keeps:
            keep.wait()
        fetch_weights(0, held % 2).start()

    @pl.when((now >= held) & more)
    def _():
        fetch_weights(coming, next_slot).start()

    @pl.when((now < 2 * held) & (turn_index < alone))
    def _():
        fetch(xa_ref.at[0], now % 2, False).wait()

        @pl.when(now < held)
        def _():
            visibility_of(False, now % 2, turn_index)

        @pl.when(now >= held)
        def _():
            fetch_weights(0, now % 2).wait()
            beams_of(False, now % 2, turn_index)
            pass_on(False, turn_index)

    @pl.when((now < 2 * held) & (turn_index >= alone))
    def _():
        fetch(xe_ref.at[0], now % 2, True).wait()

        @pl.when(now < held)
        def _():
            visibility_of(True, now % 2, turn_index - alone)

        @pl.when(now >= held)
        def _():
            fetch_weights(0, now % 2).wait()
            beams_of(True, now % 2, turn_index - alone)

        @pl.when(now == 2 * held - 1)
        def _():
            def start(step, carry):
                cell = ahead(step, 1)
                part(False, cell, me).start()

                @pl.when(cell // halves == r // half)
                def _():
                    part(True, cell, me).start()

                return carry

            lax.fori_loop(1, cells, start, 0)
            for copy in locals_:
                copy.start()

        @pl.when(now >= held)
        def _():
            pass_on(True, turn_index - alone)

    @pl.when(more & (coming >= alone + early))
    def _():
        at = coming - alone - early

        @pl.when(now < held)
        def _():
            def arrive(step, carry):
                spread(step, False, at).wait_recv()
                return carry

            lax.fori_loop(1, cs * halves, arrive, 0)

        fetch(late_ref.at[at], next_slot, True).start()

    @pl.when(now == 2 * held)
    def _():
        def finish(step, carry):
            cell = ahead(step, 1)
            row, col = cell // qs, cell % qs
            slot = ahead(step, -1)
            for kind, count in ((False, alone), (True, shared)):
                sent = jnp.logical_not(mirrored(half, r, q, row, col, kind))
                both(
                    row == col, sent, lambda planes: outgoing(kind, planes, cell, 0, count).wait_send()
                )
                passed = relayed(half, slot // qs, slot % qs, r, q, kind)

                def arrive(planes):
                    for at in range(count):
                        incoming(kind, planes, slot, at).wait_recv()

                both(r == q, jnp.logical_not(passed), arrive)

                @pl.when(passed)
                def _():
                    relay(kind, slot, 0, count).wait_send()

            part(False, cell, me).wait_send()
            part(False, me, slot).wait_recv()

            @pl.when(cell // halves == r // half)
            def _():
                part(True, cell, me).wait_send()

            @pl.when(slot // halves == r // half)
            def _():
                part(True, me, slot).wait_recv()

            return carry

        lax.fori_loop(1, cells, finish, 0)

        def left(step, carry):
            for at in range(late):
                spread(step, True, at).wait_send()
            return carry

        lax.fori_loop(1, cs * halves, left, 0)

        def sent_weights(step, carry):
            weights((q + step) % qs, q, 0, 0, held).wait_send()
            return carry

        lax.fori_loop(1, qs, sent_weights, 0)
        for copy in locals_:
            copy.wait()


def products(xa, xe, rest, weights, frames, shared):
    cs, rs, qs = sizes()
    cells = rs * qs
    halves = cells // 2
    alone, inputs, depth = xa.shape
    early = xe.shape[0]
    late = shared - early
    held = alone + shared
    beams = weights.shape[2] * qs
    bins = depth // (2 * INTEG)
    lanes = 2 * frames
    source = np.arange(lanes)[:, None]
    goal = np.arange(lanes)[None, :]
    swap = np.where(source + frames == goal, 1.0, 0.0) - np.where(source == goal + frames, 1.0, 0.0)
    at = np.arange(depth)
    frame = at // lanes * frames + at % frames
    part = bins // rs
    column = np.arange(rs * shared * part)
    bin_of = column // (shared * part) * part + column % part
    pool = np.where(frame[:, None] // INTEG == bin_of[None, :], 1.0 / INTEG, 0.0)
    anywhere = pl.BlockSpec(memory_space=pl.ANY)
    peers = cs * halves
    counts = (2, cells, cells, cells * held, cells, cells, cells, cells, cells, cells)
    counts = counts + (late * peers, late * peers, qs, qs, 2, 7)
    return pl.pallas_call(
        functools.partial(products_kernel, cs, rs, qs, depth // 2, alone, early),
        grid=(2 * held + 1,),
        out_shape=(
            jax.ShapeDtypeStruct((2, cells * held, inputs // rs, inputs // qs), jnp.bfloat16),
            jax.ShapeDtypeStruct((cells, beams // qs, shared * part), jnp.float32),
            jax.ShapeDtypeStruct((halves, beams // qs, shared * part), jnp.float32),
            jax.ShapeDtypeStruct((late, inputs, depth // 2), jnp.bfloat16),
            jax.ShapeDtypeStruct((2, held, beams, inputs), weights.dtype),
        ),
        in_specs=[
            anywhere,
            anywhere,
            anywhere,
            anywhere,
            pl.BlockSpec((lanes, lanes), lambda j: (0, 0)),
            pl.BlockSpec((depth, rs * shared * part), lambda j: (0, 0)),
        ],
        out_specs=(anywhere,) * 5,
        scratch_shapes=[
            pltpu.VMEM((2, inputs, depth), jnp.bfloat16),
            pltpu.VMEM((inputs // qs, depth), jnp.bfloat16),
            pltpu.VMEM((2, 2, beams, inputs), weights.dtype),
            pltpu.VMEM((2, held, inputs, inputs), jnp.bfloat16),
            pltpu.VMEM((beams, rs * shared * part), jnp.float32),
            pltpu.VMEM((beams, rs // 2 * shared * part), jnp.float32),
        ]
        + [pltpu.SemaphoreType.DMA((count,)) for count in counts],
        compiler_params=pltpu.CompilerParams(has_side_effects=True, vmem_limit_bytes=60 << 20),
        name="products",
    )(xa, xe, rest, weights, jnp.asarray(swap, jnp.bfloat16), jnp.asarray(pool, jnp.bfloat16))


def unpack_kernel(rs, qs, singles, one_ref, two_ref, eye_ref, out_ref):
    r, q = (lax.axis_index(name) for name in ("row", "col"))
    half = rs // 2
    step = pl.program_id(0)
    summed = step >= singles

    def turned(value):
        return lax.dot_general(
            eye_ref[...], value, (((1,), (1,)), ((), ())), preferred_element_type=jnp.float32
        )

    def straight_pair(ref, at):
        return ref[0, at].astype(jnp.float32), ref[1, at].astype(jnp.float32)

    def turned_pair(ref, at):
        return turned(ref[0, at]), -turned(ref[1, at])

    def packed_pair(ref, at):
        wide, over = ref[0, at].astype(jnp.float32), turned(ref[0, at])
        return 0.5 * (wide + over), 0.5 * (wide - over)

    def put(when, *ways):
        @pl.when(when)
        def _():
            for at in range(out_ref.shape[1]):
                re, im = ways[0](one_ref, at)
                if len(ways) > 1:
                    more_re, more_im = ways[1](two_ref, at)
                    re, im = re + more_re, im + more_im
                out_ref[0, at] = re
                out_ref[1, at] = im

    single = jnp.logical_not(summed)
    off = r != q
    over = mirrored(half, step * rs // singles, 0, r, q, False)
    put(single & (r == q), packed_pair)
    put(single & over, turned_pair)
    put(single & off & jnp.logical_not(over), straight_pair)
    col = (step - singles) % qs
    low = mirrored(half, 0, col, r, q, True)
    high = mirrored(half, half, col, r, q, True)
    put(summed & (r == q), packed_pair, packed_pair)
    put(summed & low, turned_pair, straight_pair)
    put(summed & high, straight_pair, turned_pair)
    neither = jnp.logical_not(low) & jnp.logical_not(high)
    put(summed & off & neither, straight_pair, straight_pair)


def unpack(block, alone, shared):
    _, rs, qs = sizes()
    cells = rs * qs
    singles = cells * alone // shared
    _, _, height, width = block.shape
    steps = singles + cells // 2
    shape = (2, shared, height, width)
    return pl.pallas_call(
        functools.partial(unpack_kernel, rs, qs, singles),
        grid=(steps,),
        out_shape=jax.ShapeDtypeStruct((2, steps * shared, height, width), jnp.float32),
        in_specs=[
            pl.BlockSpec(shape, lambda i: (0, i, 0, 0)),
            pl.BlockSpec(shape, lambda i: (0, jnp.maximum(i, singles) + cells // 2, 0, 0)),
            pl.BlockSpec((height, width), lambda i: (0, 0)),
        ],
        out_specs=pl.BlockSpec(shape, lambda i: (0, i, 0, 0)),
        compiler_params=pltpu.CompilerParams(vmem_limit_bytes=40 << 20),
        name="unpack",
    )(block, block, jnp.asarray(np.eye(height), jnp.bfloat16))


def by_channels(voltages, input_flags, channel_order, beam_weights):
    cs, rs, qs = sizes()
    own = NCH // (cs * rs * qs)
    alone, shared, early = own // 2, own, own // 2
    xa, xe, rest = turn(voltages, input_flags, channel_order, alone, shared, early)
    frames = voltages.shape[2] // NCH
    block, whole, halved, _, _ = products(xa, xe, rest, beam_weights, frames, shared)

    def by_position(power, count):
        sources, beams, _ = power.shape
        split = power.reshape(sources, beams, shared, -1)[:, :, :count]
        return jnp.transpose(split, (0, 2, 1, 3)).reshape(sources * count, beams, -1)

    beam_power = jnp.concatenate([by_position(whole, alone), by_position(halved, shared)], axis=0)
    return (unpack(block, alone, shared), beam_power)


def on_device(voltages, input_flags, channel_order, beam_weights):
    cs, rs, qs = sizes()
    lanes = 2 * (voltages.shape[2] // NCH)
    devices = cs * rs * qs
    square = rs == qs and rs % 2 == 0 and NCH // devices % 2 == 0
    whole = square and NCH % devices == 0 and lanes % 128 == 0 and voltages.shape[1] % 16 == 0
    if whole and NCH // devices * (lanes // 2 * qs // INTEG) % 128 == 0:
        plan = by_channels
    else:
        plan = by_panels
    return plan(voltages, input_flags, channel_order, beam_weights)


def solution(mesh):
    placed = (P(None, "chan", ("row", "col")), P("chan"), P(), P(None, "chan", "col", None))
    return jax.shard_map(
        on_device,
        mesh=mesh,
        in_specs=placed,
        out_specs=(P(None, "chan", "row", "col"), P("chan", "col", "row")),
        check_vma=False,
    )
```

```python
import functools
import math

import jax
import jax.numpy as jnp
import numpy as np
from jax import lax
from jax.experimental import pallas as pl
from jax.experimental.pallas import tpu as pltpu
from jax.sharding import PartitionSpec as P

NCH = 128
TAPS = 4
INTEG = 8


def passed_along(value, axis, steps):
    count = lax.axis_size(axis)
    initial, last = (max(0, -steps), min(count, count - steps))
    return lax.ppermute(value, axis, [(source, source + steps) for source in range(initial, last)])


def prototype(taps, length):
    position = jnp.arange(taps * length, dtype=jnp.float32) + 0.5
    offset = position / length - taps / 2.0
    window = 0.5 - 0.5 * jnp.cos(2.0 * math.pi * position / (taps * length))
    return (jnp.sin(math.pi * offset) / (math.pi * offset) * window).reshape(taps, length)


def dft_tables(channel_rows, length):
    sample_index = jnp.arange(length, dtype=jnp.int32)
    product = channel_rows[:, None] * sample_index[None, :] % length
    angle = 2.0 * math.pi / length * product.astype(jnp.float32)
    factor = 1.0 / math.sqrt(length)
    cosine = jnp.cos(angle) * factor
    sine = jnp.sin(angle) * factor
    real_rows = jnp.stack([cosine, sine], axis=1)
    imag_rows = jnp.stack([-sine, cosine], axis=1)
    return jnp.stack([real_rows, imag_rows], axis=1).astype(jnp.bfloat16)


def to_frames(gathered, frames, outer, inner, swapped):
    chans = gathered.shape[0]
    width = gathered.shape[1]
    split = gathered.reshape(chans, width, outer, inner, 2, frames)
    if swapped:
        order = jnp.transpose(split, (0, 4, 1, 3, 2, 5))
    else:
        order = jnp.transpose(split, (0, 4, 1, 2, 3, 5))
    return order.reshape(chans, 2, width, outer * inner * frames)


def correlate_one(left_block, right_block, frame_count):
    left_re = left_block[0]
    left_im = left_block[1]
    right_re = right_block[0]
    right_im = right_block[1]
    dims = (((1,), (1,)), ((), ()))
    vis_re = lax.dot_general(left_re, right_re, dims, preferred_element_type=jnp.float32)
    vis_re = vis_re + lax.dot_general(left_im, right_im, dims, preferred_element_type=jnp.float32)
    vis_im = lax.dot_general(left_im, right_re, dims, preferred_element_type=jnp.float32)
    vis_im = vis_im - lax.dot_general(left_re, right_im, dims, preferred_element_type=jnp.float32)
    return jnp.stack([vis_re, vis_im]) / frame_count


def correlate(left_view, right_view, frame_count):
    result = lax.map(
        lambda items: correlate_one(items[0], items[1], frame_count), (left_view, right_view)
    )
    return jnp.transpose(result, (1, 0, 2, 3))


def beams_one(weights, block):
    w_real = weights[0]
    w_imag = weights[1]
    x_real = block[0]
    x_imag = block[1]
    beam_re = jnp.dot(w_real, x_real, preferred_element_type=jnp.float32) - jnp.dot(
        w_imag, x_imag, preferred_element_type=jnp.float32
    )
    beam_im = jnp.dot(w_real, x_imag, preferred_element_type=jnp.float32) + jnp.dot(
        w_imag, x_real, preferred_element_type=jnp.float32
    )
    return jnp.stack([beam_re, beam_im], axis=1)


def form_beams(weights, view):
    by_channel = jnp.transpose(weights, (1, 0, 2, 3))
    return lax.map(lambda items: beams_one(items[0], items[1]), (by_channel, view))


def integrate(voltage):
    power = voltage[:, :, 0] * voltage[:, :, 0] + voltage[:, :, 1] * voltage[:, :, 1]
    return power.reshape(power.shape[0], power.shape[1], -1, INTEG).mean(axis=-1)


def channelize(voltages, input_flags, channel_order):
    masked = voltages * input_flags.astype(jnp.bfloat16)[None, :, None]
    local_inputs = masked.shape[1]
    frames = masked.shape[2] // NCH
    history = passed_along(masked[:, :, masked.shape[2] - (TAPS - 1) * NCH :], ("row", "col"), 1)
    joined = jnp.concatenate([history, masked], axis=2)
    blocks = joined.reshape(2, local_inputs, frames + TAPS - 1, NCH)
    coeffs = prototype(TAPS, NCH)
    filtered = jnp.zeros((2, local_inputs, frames, NCH), jnp.float32)
    for tap_index in range(TAPS):
        filtered = filtered + coeffs[tap_index] * blocks[
            :, :, tap_index : tap_index + frames
        ].astype(jnp.float32)
    filtered = filtered.astype(jnp.bfloat16)
    tables = dft_tables(channel_order, NCH)
    spectrum = jnp.einsum(
        "kqpn,pifn->kiqf",
        tables.astype(jnp.float32),
        filtered.astype(jnp.float32),
        precision=lax.Precision.HIGHEST,
    ).astype(jnp.bfloat16)
    spectrum = spectrum.reshape(NCH, local_inputs, 2 * frames)
    return spectrum


def by_panels(voltages, input_flags, channel_order, beam_weights):
    spectrum = channelize(voltages, input_flags, channel_order)
    frames = spectrum.shape[2] // 2
    turned = lax.all_to_all(spectrum, "chan", split_axis=0, concat_axis=1, tiled=True)
    row_count = lax.axis_size("row")
    col_count = lax.axis_size("col")
    total_frames = frames * row_count * col_count
    row_turned = lax.all_to_all(turned, "row", split_axis=1, concat_axis=2, tiled=True)
    row_all = lax.all_gather(row_turned, "col", axis=2, tiled=True)
    col_turned = lax.all_to_all(turned, "col", split_axis=1, concat_axis=2, tiled=True)
    col_all = lax.all_gather(col_turned, "row", axis=2, tiled=True)
    row_view = to_frames(row_all, frames, col_count, row_count, True)
    col_view = to_frames(col_all, frames, row_count, col_count, False)
    visibility = correlate(row_view, col_view, total_frames)
    weights_all = lax.all_gather(beam_weights, "col", axis=2, tiled=True)
    local_view = to_frames(turned, frames, 1, 1, False)
    voltage = form_beams(weights_all, local_view)
    own_power = integrate(voltage)
    beam_power = lax.all_to_all(own_power, "col", split_axis=1, concat_axis=2, tiled=True)
    return (visibility, beam_power)


MESH = pl.DeviceIdType.MESH


def spectra_tile(v_ref, h_ref, flag_ref, coeff_ref, table_ref, filtered_ref, wide_ref):
    tile = v_ref.shape[1]
    frames = v_ref.shape[2] // NCH
    lanes = 2 * frames
    flag = jnp.broadcast_to(flag_ref[...], (tile, NCH))
    rows = [jnp.broadcast_to(coeff_ref[tap : tap + 1, :], (tile, NCH)) for tap in range(TAPS)]
    for part in range(2):

        def frame_at(index):
            ref, at = (h_ref, index) if index < TAPS - 1 else (v_ref, index - TAPS + 1)
            return ref[part, :, at * NCH : (at + 1) * NCH].astype(jnp.float32) * flag

        window = [frame_at(index) for index in range(TAPS - 1)]
        for frame in range(frames):
            window = window[-(TAPS - 1) :] + [frame_at(frame + TAPS - 1)]
            total = rows[0] * window[0]
            for tap in range(1, TAPS):
                total = total + rows[tap] * window[tap]
            filtered_ref[part, frame] = total
    for first in range(0, tile, 2):
        stack = []
        for index in (first, first + 1):
            re = filtered_ref[0, :, index, :].astype(jnp.bfloat16)
            im = filtered_ref[1, :, index, :].astype(jnp.bfloat16)
            stack.append(jnp.concatenate([re, im], axis=1))
            stack.append(jnp.concatenate([im, -re], axis=1))
        both = lax.dot_general(
            table_ref[...],
            jnp.concatenate(stack, axis=0),
            (((1,), (1,)), ((), ())),
            preferred_element_type=jnp.float32,
        )
        wide_ref[:, first, :] = both[:, :lanes]
        wide_ref[:, first + 1, :] = both[:, lanes:]
    return wide_ref[...].astype(jnp.bfloat16)


def sizes():
    return lax.axis_size("chan"), lax.axis_size("row"), lax.axis_size("col")


def part_of(c, r, q, cs, half, qs, step):
    inner = step // cs
    row = r // half * half + (r % half + inner % half) % half
    return (c + step % cs) % cs, row, (q + inner // half) % qs


def turn_kernel(
    cs, rs, qs, tile, group, wide, alone, early,
    v_ref, flag_ref, coeff_ref, table_ref, whole_ref, x_ref, e_ref, s_ref,
    filtered_ref, wide_ref, spec_ref, past_ref, send, recv, psend, precv, local,
):
    c, r, q = (lax.axis_index(name) for name in ("chan", "row", "col"))
    half = rs // 2
    cells = rs * qs
    halves = half * qs
    devices = cs * cells
    me = r * qs + q
    mine = me % halves
    here = c * cells + me
    inputs = spec_ref.shape[1]
    lanes = spec_ref.shape[2]
    early_base = devices * alone
    late_base = early_base + cs * halves * early
    turn_step = pl.program_id(0)
    tiles = inputs // tile

    def ahead(step):
        return (r + step % rs) % rs * qs + (q + step // rs) % qs

    def rows_at(first, count):
        return pl.ds(pl.multiple_of(first, tile), count)

    def spectra(step, first, count):
        chan, cell = (c + step % cs) % cs, ahead(step // cs)
        origin, column = c, me
        return pltpu.make_async_remote_copy(
            src_ref=spec_ref.at[
                pl.ds((chan * cells + cell) * alone, alone), rows_at(first, count)
            ],
            dst_ref=x_ref.at[
                :,
                rows_at(origin * inputs + first, count),
                pl.ds(pl.multiple_of(column * lanes, lanes), lanes),
            ],
            send_sem=send.at[0],
            recv_sem=recv.at[0],
            device_id=(chan, cell // qs, cell % qs),
            device_id_type=MESH,
        )

    def sooner(step, first, count):
        chan, row, col = part_of(c, r, q, cs, half, qs, step)
        place = row % half * qs + col
        origin, column = c, mine
        return pltpu.make_async_remote_copy(
            src_ref=spec_ref.at[
                pl.ds(early_base + (chan * halves + place) * early, early), rows_at(first, count)
            ],
            dst_ref=e_ref.at[
                :,
                rows_at(origin * inputs + first, count),
                pl.ds(pl.multiple_of(column * lanes, lanes), lanes),
            ],
            send_sem=send.at[1],
            recv_sem=recv.at[1],
            device_id=(chan, row, col),
            device_id_type=MESH,
        )

    past = past_ref.shape[2]
    chunk = tile if inputs % wide else wide

    def last_frames(first):
        following = (me + 1) % cells
        rows = rows_at(first, chunk)
        return pltpu.make_async_remote_copy(
            src_ref=whole_ref.at[:, rows, pl.ds(whole_ref.shape[2] - past, past)],
            dst_ref=past_ref.at[:, rows],
            send_sem=psend.at[0],
            recv_sem=precv.at[first // chunk],
            device_id=(c, following // qs, following % qs),
            device_id_type=MESH,
        )

    @pl.when((turn_step == 0) & (me + 1 < cells))
    def _():
        for first in range(0, inputs, chunk):
            last_frames(first).start()

    @pl.when((turn_step == 0) & (me == 0))
    def _():
        past_ref[...] = jnp.zeros_like(past_ref)

    @pl.when((turn_step < tiles) & (me > 0) & (turn_step * tile % chunk == 0))
    def _():
        last_frames(turn_step * tile).wait_recv()

    @pl.when((turn_step == tiles) & (me + 1 < cells))
    def _():
        pltpu.make_async_remote_copy(
            src_ref=past_ref,
            dst_ref=past_ref,
            send_sem=psend.at[0],
            recv_sem=precv.at[0],
            device_id=(c, r, q),
            device_id_type=MESH,
        ).wait_send()

    @pl.when((turn_step > 0) & (turn_step * tile % group == 0))
    def _():
        def start(step, carry):
            spectra(step, turn_step * tile - group, group).start()
            return carry

        lax.fori_loop(1, devices, start, 0)

    @pl.when((turn_step > 0) & (turn_step * tile % wide == 0))
    def _():
        def start(step, carry):
            sooner(step, turn_step * tile - wide, wide).start()
            return carry

        lax.fori_loop(1, cs * halves, start, 0)

    @pl.when(turn_step < tiles)
    def _():
        at = pl.ds(pl.multiple_of(turn_step * tile, tile), tile)
        spec_ref[:, at, :] = spectra_tile(
            v_ref, past_ref.at[:, at], flag_ref, coeff_ref, table_ref, filtered_ref, wide_ref
        )

    @pl.when(turn_step == tiles)
    def _():
        stays = [
            pltpu.make_async_copy(
                spec_ref.at[pl.ds(here * alone, alone)],
                x_ref.at[
                    :, rows_at(c * inputs, inputs), pl.ds(pl.multiple_of(me * lanes, lanes), lanes)
                ],
                local.at[0],
            ),
            pltpu.make_async_copy(
                spec_ref.at[pl.ds(early_base + (c * halves + mine) * early, early)],
                e_ref.at[
                    :,
                    rows_at(c * inputs, inputs),
                    pl.ds(pl.multiple_of(mine * lanes, lanes), lanes),
                ],
                local.at[1],
            ),
            pltpu.make_async_copy(
                spec_ref.at[pl.ds(late_base, s_ref.shape[0])], s_ref, local.at[2]
            ),
        ]
        for stay in stays:
            stay.start()

        for index, count in enumerate(((devices - 1) * alone, (cs * halves - 1) * early)):
            rows = spec_ref.at[pl.ds(0, count)]
            every = pltpu.make_async_remote_copy(
                src_ref=rows,
                dst_ref=rows,
                send_sem=send.at[index],
                recv_sem=recv.at[index],
                device_id=(c, r, q),
                device_id_type=MESH,
            )
            every.wait_send()
            every.wait_recv()
        for stay in stays:
            stay.wait()


def turn(voltages, input_flags, channel_order, alone, shared, early):
    cs, rs, qs = sizes()
    devices = cs * rs * qs
    halves = rs // 2 * qs
    _, inputs, samples = voltages.shape
    past = (TAPS - 1) * NCH
    frames = samples // NCH
    lanes = 2 * frames
    tile = 16
    group = 2 * tile if inputs % (2 * tile) == 0 else tile
    wide = 4 * group if inputs % (4 * group) == 0 else group
    last = inputs // tile - 1
    place = jnp.arange(NCH).reshape(cs, NCH // cs)
    split = place[:, rs * qs * alone :].reshape(cs, halves, shared)
    order = jnp.concatenate(
        [
            place[:, : rs * qs * alone].reshape(-1),
            split[:, :, :early].reshape(-1),
            split[:, :, early:].reshape(-1),
        ]
    )
    tables = dft_tables(channel_order[order], NCH)[:, 0].reshape(NCH, 2 * NCH)
    anywhere = pl.BlockSpec(memory_space=pl.ANY)
    counts = (2, 2, 1, inputs // tile, 3)
    return pl.pallas_call(
        functools.partial(turn_kernel, cs, rs, qs, tile, group, wide, alone, early),
        grid=(inputs // tile + 1,),
        out_shape=(
            jax.ShapeDtypeStruct((alone, inputs * cs, lanes * rs * qs), jnp.bfloat16),
            jax.ShapeDtypeStruct((early, inputs * cs, lanes * halves), jnp.bfloat16),
            jax.ShapeDtypeStruct((cs * halves * (shared - early), inputs, lanes), jnp.bfloat16),
        ),
        in_specs=[
            pl.BlockSpec((2, tile, samples), lambda i: (0, jnp.minimum(i, last), 0)),
            pl.BlockSpec((tile, 1), lambda i: (jnp.minimum(i, last), 0)),
            pl.BlockSpec((TAPS, NCH), lambda i: (0, 0)),
            pl.BlockSpec((NCH, 2 * NCH), lambda i: (0, 0)),
            anywhere,
        ],
        out_specs=(anywhere,) * 3,
        scratch_shapes=[
            pltpu.VMEM((2, frames, tile, NCH), jnp.float32),
            pltpu.VMEM((NCH, tile, lanes), jnp.float32),
            pltpu.VMEM((NCH, inputs, lanes), jnp.bfloat16),
            pltpu.VMEM((2, inputs, past), jnp.bfloat16),
        ]
        + [pltpu.SemaphoreType.DMA((count,)) for count in counts],
        compiler_params=pltpu.CompilerParams(has_side_effects=True, vmem_limit_bytes=60 << 20),
        name="turn",
    )(
        voltages,
        input_flags.astype(jnp.float32)[:, None],
        prototype(TAPS, NCH),
        tables,
        voltages,
    )


def crosses(half, source_row, row, col):
    return (row != col) & (row // half == col // half) & (source_row // half != row // half)


def nearer(half, row, col):
    upper = row // half == 1
    return (upper & (row < col)) | (jnp.logical_not(upper) & (row > col))


def mirrored(half, source_row, row, col):
    return crosses(half, source_row, row, col) & jnp.logical_not(nearer(half, row, col))


def products_kernel(
    cs, rs, qs, frame_count, alone, early,
    xa_ref, xe_ref, s_ref, weight_ref, swap_ref, pool_ref,
    block_ref, parta_ref, partb_ref, late_ref, all_ref, stage_ref,
    x_ref, y_ref, w_ref, vis_ref, powera_ref, powerb_ref,
    load, send, recv, stage_send, stage_recv, relay_send,
    psend, precv, lsend, lrecv, wsend, wrecv, wload, local,
):
    c, r, q = (lax.axis_index(name) for name in ("chan", "row", "col"))
    cells = rs * qs
    half = rs // 2
    halves = half * qs
    me = r * qs + q
    mine = me % halves
    held, inputs = vis_ref.shape[1], vis_ref.shape[2]
    shared = held - alone
    late = shared - early
    depth = x_ref.shape[2]
    depths = {False: depth, True: depth // 2}
    lanes = swap_ref.shape[0]
    own_inputs = inputs // cs
    height, width = block_ref.shape[2], block_ref.shape[3]
    part_height, part_width = parta_ref.shape[1], parta_ref.shape[2]
    now = pl.program_id(0)

    def ahead(step, sign):
        row = (r + rs + sign * (step % rs)) % rs
        return row * qs + (q + qs + sign * (step // rs)) % qs

    def vis_at(planes, first, count, row, col):
        return vis_ref.at[
            pl.ds(0, planes),
            pl.ds(first, count),
            pl.ds(pl.multiple_of(row * height, height), height),
            pl.ds(pl.multiple_of(col * width, width), width),
        ]

    def power_at(ref, row, col):
        return ref.at[
            pl.ds(pl.multiple_of(col * part_height, part_height), part_height),
            pl.ds(pl.multiple_of(row * part_width, part_width), part_width),
        ]

    def landing(kind, planes, cell, first, count):
        base = cells * alone + cell * shared if kind else cell * alone
        return block_ref.at[pl.ds(0, planes), pl.ds(base + first, count)]

    def outgoing(kind, planes, cell, first, count):
        return pltpu.make_async_remote_copy(
            src_ref=vis_at(planes, first + (alone if kind else 0), count, cell // qs, cell % qs),
            dst_ref=landing(kind, planes, me, first, count),
            send_sem=send.at[planes - 1],
            recv_sem=recv.at[0],
            device_id=(c, cell // qs, cell % qs),
            device_id_type=MESH,
        )

    def together(rows, leaves, comes):
        return pltpu.make_async_remote_copy(
            src_ref=rows,
            dst_ref=rows,
            send_sem=leaves,
            recv_sem=comes,
            device_id=(c, r, q),
            device_id_type=MESH,
        )

    def staged(pair, row, first, count):
        return stage_ref.at[:, pl.ds((pair * half + row % half) * held + first, count)]

    def to_relay(row, col, first, count):
        inner = jnp.where(r < half, row - half, half - 1 - row)
        outer = jnp.where(r < half, col - half, half - 1 - col)
        pair = inner * (2 * half - inner - 1) // 2 + outer - inner - 1
        return pltpu.make_async_remote_copy(
            src_ref=vis_at(2, first, count, row, col),
            dst_ref=staged(pair, r, first, count),
            send_sem=stage_send.at[0],
            recv_sem=stage_recv.at[(pair * half + r % half) * held + first],
            device_id=(c, jnp.where(r < half, half, half - 1), q),
            device_id_type=MESH,
        )

    def at_relay(pair, row, first):
        return pltpu.make_async_remote_copy(
            src_ref=staged(pair, row, first, 1),
            dst_ref=staged(pair, row, first, 1),
            send_sem=stage_send.at[0],
            recv_sem=stage_recv.at[(pair * half + row % half) * held + first],
            device_id=(c, row, q),
            device_id_type=MESH,
        )

    def from_relay(kind, pair, row, at, first, count, goal):
        return pltpu.make_async_remote_copy(
            src_ref=staged(pair, row, first, count),
            dst_ref=landing(kind, 2, row * qs + q, at, count),
            send_sem=relay_send.at[0],
            recv_sem=recv.at[0],
            device_id=(c,) + goal,
            device_id_type=MESH,
        )

    relays = r == jnp.where(r < half, half - 1, half)
    pairs = [(inner, outer) for inner in range(half) for outer in range(inner + 1, half)]

    def owners(pair):
        inner, outer = pairs[pair]
        row = jnp.where(r < half, half - 1 - inner, half + inner)
        col = jnp.where(r < half, half - 1 - outer, half + outer)
        return row, col

    def both(diagonal, sent, act):
        @pl.when(sent & diagonal)
        def _():
            act(1)

        @pl.when(sent & jnp.logical_not(diagonal))
        def _():
            act(2)

    def part(kind, cell, slot):
        source, goal = (powerb_ref, partb_ref) if kind else (powera_ref, parta_ref)
        row = cell // qs % half if kind else cell // qs
        place = slot % halves if kind else slot
        return pltpu.make_async_remote_copy(
            src_ref=power_at(source, row, cell % qs),
            dst_ref=goal.at[place],
            send_sem=psend.at[1 if kind else 0],
            recv_sem=precv.at[1 if kind else 0],
            device_id=(c, cell // qs, cell % qs),
            device_id_type=MESH,
        )

    peers = cs * halves

    def spread(step, at):
        chan, row, col = part_of(c, r, q, cs, half, qs, step)
        place = row % half * qs + col
        origin, column = c, mine
        return pltpu.make_async_remote_copy(
            src_ref=s_ref.at[(chan * halves + place) * late + at],
            dst_ref=late_ref.at[
                at,
                pl.ds(pl.multiple_of(origin * own_inputs, own_inputs), own_inputs),
                pl.ds(pl.multiple_of(column * lanes, lanes), lanes),
            ],
            send_sem=lsend.at[0],
            recv_sem=lrecv.at[at],
            device_id=(chan, row, col),
            device_id_type=MESH,
        )

    def stay_late(at):
        return pltpu.make_async_copy(
            s_ref.at[(c * halves + mine) * late + at],
            late_ref.at[
                at,
                pl.ds(pl.multiple_of(c * own_inputs, own_inputs), own_inputs),
                pl.ds(pl.multiple_of(mine * lanes, lanes), lanes),
            ],
            local.at[4],
        )

    def fetch(source, slot, kind):
        return pltpu.make_async_copy(
            source, x_ref.at[slot, :, pl.ds(0, depths[kind])], load.at[slot]
        )

    def weight_spans(peer):
        cell = r * qs + peer
        return (
            (cell * alone, 0, alone),
            (cells * alone + cell % halves * shared, alone, shared),
        )

    def weights_at(slot, goal, count):
        beams = weight_ref.shape[2]
        return all_ref.at[
            :, pl.ds(goal, count), pl.ds(pl.multiple_of(slot * beams, beams), beams)
        ]

    def weights(peer, slot, source, goal, count):
        return pltpu.make_async_remote_copy(
            src_ref=weight_ref.at[:, pl.ds(source, count)],
            dst_ref=weights_at(slot, goal, count),
            send_sem=wsend.at[peer],
            recv_sem=wrecv.at[slot],
            device_id=(c, r, peer),
            device_id_type=MESH,
        )

    keeps = [
        pltpu.make_async_copy(
            weight_ref.at[:, pl.ds(source, count)], weights_at(q, goal, count), local.at[5 + index]
        )
        for index, (source, goal, count) in enumerate(weight_spans(q))
    ]

    def fetch_weights(index, slot):
        return pltpu.make_async_copy(all_ref.at[:, index], w_ref.at[slot], wload.at[slot])

    def visibility_of(kind, slot, at):
        deep = depths[kind]
        across = (((1,), (1,)), ((), ()))
        index = at + (alone if kind else 0)

        def panels(step, carry):
            col = (q + step) % qs
            span = pl.ds(pl.multiple_of(col * width, width), width)
            for start in range(0, deep, lanes):
                y_ref[:, start : start + lanes] = jnp.dot(
                    x_ref[slot, span, start : start + lanes],
                    swap_ref[...],
                    preferred_element_type=jnp.float32,
                ).astype(jnp.bfloat16)
            every = x_ref[slot, :, :deep]
            re = lax.dot_general(
                every, x_ref[slot, span, :deep], across, preferred_element_type=jnp.float32
            )
            im = lax.dot_general(every, y_ref[:, :deep], across, preferred_element_type=jnp.float32)
            panel = lax.broadcasted_iota(jnp.int32, re.shape, 0) // height
            first = jnp.where(panel == col, re + im, re)
            vis_ref[0, index, :, span] = (first / frame_count).astype(vis_ref.dtype)
            vis_ref[1, index, :, span] = (im / frame_count).astype(vis_ref.dtype)

            def start(step, carry):
                outward = jnp.where(step % 2 == 0, half + step // 2, half - 1 - step // 2)
                row = jnp.where(r < half, outward, rs - 1 - outward)
                cell = row * qs + col
                shared_pair = crosses(half, r, row, col)
                sent = (cell != me) & jnp.logical_not(shared_pair)
                both(row == col, sent, lambda planes: outgoing(kind, planes, cell, at, 1).start())

                @pl.when(shared_pair & nearer(half, row, col))
                def _():
                    to_relay(row, col, index, 1).start()

                return carry

            lax.fori_loop(0, rs, start, 0)
            return carry

        lax.fori_loop(0, qs, panels, 0)

    def beams_of(kind, slot, at):
        deep = depths[kind]
        span = 4 * lanes if deep % (4 * lanes) == 0 else lanes
        power_ref = powerb_ref if kind else powera_ref
        columns_out = power_ref.shape[1]
        middle = lanes // 2

        def columns(step, carry):
            along = pl.ds(pl.multiple_of(step * span, span), span)
            x = x_ref[slot, :, along]
            straight = jnp.dot(w_ref[slot, 0], x, preferred_element_type=jnp.float32)
            crossed = jnp.dot(w_ref[slot, 1], x, preferred_element_type=jnp.float32)
            swapped = []
            for start in range(0, span, lanes):
                swapped.append(crossed[:, start + middle : start + lanes])
                swapped.append(-crossed[:, start : start + middle])
            beam = straight - jnp.concatenate(swapped, axis=1)
            square = beam * beam
            high = square.astype(jnp.bfloat16)
            low = (square - high.astype(jnp.float32)).astype(jnp.bfloat16)
            pool = pool_ref[along, :columns_out]
            return (
                carry
                + jnp.dot(high, pool, preferred_element_type=jnp.float32)
                + jnp.dot(low, pool, preferred_element_type=jnp.float32)
            )

        found = lax.fori_loop(0, deep // span, columns, jnp.zeros(power_ref.shape, jnp.float32))
        lane = lax.broadcasted_iota(jnp.int32, power_ref.shape, 1) % part_width
        power_ref[...] = jnp.where(lane // (part_width // shared) == at, found, power_ref[...])

    def pass_on(kind, at):
        index = at + (alone if kind else 0)

        @pl.when(relays)
        def _():
            for pair in range(len(pairs)):
                row, col = owners(pair)

                def one(step, carry, pair=pair, row=row, col=col):
                    source = (1 - r // half) * half + step
                    at_relay(pair, source, index).wait_recv()
                    from_relay(kind, pair, source, at, index, 1, (col, row)).start()
                    mine_too = (row == r) & (col == q)

                    @pl.when(mine_too)
                    def _():
                        pltpu.make_async_copy(
                            staged(pair, source, index, 1),
                            landing(kind, 2, source * qs + q, at, 1),
                            recv.at[0],
                        ).start()

                    @pl.when(jnp.logical_not(mine_too))
                    def _():
                        from_relay(kind, pair, source, at, index, 1, (row, col)).start()

                    return carry

                lax.fori_loop(0, half, one, 0)

    locals_ = [
        pltpu.make_async_copy(
            vis_at(2, 0, alone, r, q), landing(False, 2, me, 0, alone), local.at[0]
        ),
        pltpu.make_async_copy(
            vis_at(2, alone, shared, r, q), landing(True, 2, me, 0, shared), local.at[1]
        ),
        pltpu.make_async_copy(power_at(powera_ref, r, q), parta_ref.at[me], local.at[2]),
        pltpu.make_async_copy(power_at(powerb_ref, r % half, q), partb_ref.at[mine], local.at[3]),
    ]
    coming = (now + 1) % held
    next_slot = (now + 1) % 2
    more = now + 1 < 2 * held
    turn_index = now % held

    @pl.when(now == 0)
    def _():
        powera_ref[...] = jnp.zeros_like(powera_ref)
        powerb_ref[...] = jnp.zeros_like(powerb_ref)
        fetch(xa_ref.at[0], 0, False).start()

    @pl.when(now < late)
    def _():
        def start(step, carry):
            spread(step, now).start()
            return carry

        lax.fori_loop(1, cs * halves, start, 0)
        stay = stay_late(now)
        stay.start()
        stay.wait()

    @pl.when(now == late)
    def _():
        def start(step, carry):
            peer = (q + step) % qs
            for source, goal, count in weight_spans(peer):
                weights(peer, q, source, goal, count).start()
            return carry

        lax.fori_loop(1, qs, start, 0)
        for keep in keeps:
            keep.start()

    @pl.when(more & (coming < alone))
    def _():
        fetch(xa_ref.at[coming], next_slot, False).start()

    @pl.when(more & (coming >= alone) & (coming < alone + early))
    def _():
        fetch(xe_ref.at[coming - alone], next_slot, True).start()

    @pl.when(now == held)
    def _():
        def arrive(step, carry):
            behind = (q + qs - step) % qs
            weights(behind, behind, 0, 0, held).wait_recv()
            return carry

        lax.fori_loop(1, qs, arrive, 0)
        for keep in keeps:
            keep.wait()
        fetch_weights(0, held % 2).start()

    @pl.when((now >= held) & more)
    def _():
        fetch_weights(coming, next_slot).start()

    @pl.when((now < 2 * held) & (turn_index < alone))
    def _():
        fetch(xa_ref.at[0], now % 2, False).wait()

        @pl.when(now < held)
        def _():
            visibility_of(False, now % 2, turn_index)

        @pl.when(now >= held)
        def _():
            fetch_weights(0, now % 2).wait()
            beams_of(False, now % 2, turn_index)
            pass_on(False, turn_index)

    @pl.when((now < 2 * held) & (turn_index >= alone))
    def _():
        fetch(xe_ref.at[0], now % 2, True).wait()

        @pl.when(now < held)
        def _():
            visibility_of(True, now % 2, turn_index - alone)

        @pl.when(now >= held)
        def _():
            fetch_weights(0, now % 2).wait()
            beams_of(True, now % 2, turn_index - alone)

        @pl.when(now == 2 * held - 1)
        def _():
            def start(step, carry):
                cell = ahead(step, 1)
                part(False, cell, me).start()

                @pl.when(cell // halves == r // half)
                def _():
                    part(True, cell, me).start()

                return carry

            lax.fori_loop(1, cells, start, 0)
            for copy in locals_:
                copy.start()

        @pl.when(now >= held)
        def _():
            pass_on(True, turn_index - alone)

    @pl.when(more & (coming >= alone + early))
    def _():
        at = coming - alone - early

        @pl.when(now < held)
        def _():
            together(s_ref.at[pl.ds(0, peers - 1)], lsend.at[0], lrecv.at[at]).wait_recv()

        fetch(late_ref.at[at], next_slot, True).start()

    @pl.when(now == 2 * held)
    def _():
        plain = cells - 1 - rs - 2 * len(pairs)

        def sent(diagonal, straight):
            for planes, count in ((1, diagonal), (2, straight)):
                rows = block_ref.at[pl.ds(0, planes), pl.ds(0, count * held)]
                together(rows, send.at[planes - 1], recv.at[0]).wait_send()

        @pl.when(r == q)
        def _():
            sent(rs - 1, plain + 1)
            rows = block_ref.at[pl.ds(0, 1), pl.ds(0, (cells - 1) * held)]
            together(rows, send.at[0], recv.at[0]).wait_recv()

        @pl.when(r != q)
        def _():
            sent(rs, plain)
            rows = block_ref.at[pl.ds(0, 2), pl.ds(0, (cells - 1) * held)]
            together(rows, send.at[0], recv.at[0]).wait_recv()

        rows = block_ref.at[pl.ds(0, 2), pl.ds(0, len(pairs) * held)]
        together(rows, stage_send.at[0], recv.at[0]).wait_send()
        for index, (ref, count) in enumerate(((parta_ref, cells - 1), (partb_ref, halves - 1))):
            every = together(ref.at[pl.ds(0, count)], psend.at[index], precv.at[index])
            every.wait_send()
            every.wait_recv()

        @pl.when(relays)
        def _():
            own = jnp.where(r < half, r > q, r < q) & (r // half == q // half)
            all_passed = 2 * len(pairs) * half * held

            def passed(count):
                rows = block_ref.at[pl.ds(0, 2), pl.ds(0, count)]
                together(rows, relay_send.at[0], recv.at[0]).wait_send()

            @pl.when(own)
            def _():
                passed(all_passed - half * held)

            @pl.when(jnp.logical_not(own))
            def _():
                passed(all_passed)

        together(s_ref.at[pl.ds(0, late * (peers - 1))], lsend.at[0], lrecv.at[0]).wait_send()

        def sent_weights(step, carry):
            weights((q + step) % qs, q, 0, 0, held).wait_send()
            return carry

        lax.fori_loop(1, qs, sent_weights, 0)
        for copy in locals_:
            copy.wait()


def products(xa, xe, rest, weights, frames, shared):
    cs, rs, qs = sizes()
    cells = rs * qs
    halves = cells // 2
    alone, inputs, depth = xa.shape
    early = xe.shape[0]
    late = shared - early
    held = alone + shared
    beams = weights.shape[2] * qs
    bins = depth // (2 * INTEG)
    lanes = 2 * frames
    source = np.arange(lanes)[:, None]
    goal = np.arange(lanes)[None, :]
    swap = np.where(source + frames == goal, 1.0, 0.0) - np.where(source == goal + frames, 1.0, 0.0)
    at = np.arange(depth)
    frame = at // lanes * frames + at % frames
    part = bins // rs
    column = np.arange(rs * shared * part)
    bin_of = column // (shared * part) * part + column % part
    pool = np.where(frame[:, None] // INTEG == bin_of[None, :], 1.0 / INTEG, 0.0)
    anywhere = pl.BlockSpec(memory_space=pl.ANY)
    half = rs // 2
    pairs = half * (half - 1) // 2
    stages = pairs * half * held
    counts = (2, 2, 1, 1, stages, 1, 2, 2, 1, late, qs, qs, 2, 7)
    return pl.pallas_call(
        functools.partial(products_kernel, cs, rs, qs, depth // 2, alone, early),
        grid=(2 * held + 1,),
        out_shape=(
            jax.ShapeDtypeStruct((2, cells * held, inputs // rs, inputs // qs), jnp.bfloat16),
            jax.ShapeDtypeStruct((cells, beams // qs, shared * part), jnp.float32),
            jax.ShapeDtypeStruct((halves, beams // qs, shared * part), jnp.float32),
            jax.ShapeDtypeStruct((late, inputs, depth // 2), jnp.bfloat16),
            jax.ShapeDtypeStruct((2, held, beams, inputs), weights.dtype),
            jax.ShapeDtypeStruct((2, stages, inputs // rs, inputs // qs), jnp.bfloat16),
        ),
        in_specs=[
            anywhere,
            anywhere,
            anywhere,
            anywhere,
            pl.BlockSpec((lanes, lanes), lambda j: (0, 0)),
            pl.BlockSpec((depth, rs * shared * part), lambda j: (0, 0)),
        ],
        out_specs=(anywhere,) * 6,
        scratch_shapes=[
            pltpu.VMEM((2, inputs, depth), jnp.bfloat16),
            pltpu.VMEM((inputs // qs, depth), jnp.bfloat16),
            pltpu.VMEM((2, 2, beams, inputs), weights.dtype),
            pltpu.VMEM((2, held, inputs, inputs), jnp.bfloat16),
            pltpu.VMEM((beams, rs * shared * part), jnp.float32),
            pltpu.VMEM((beams, rs // 2 * shared * part), jnp.float32),
        ]
        + [pltpu.SemaphoreType.DMA((count,)) for count in counts],
        compiler_params=pltpu.CompilerParams(has_side_effects=True, vmem_limit_bytes=60 << 20),
        name="products",
    )(xa, xe, rest, weights, jnp.asarray(swap, jnp.bfloat16), jnp.asarray(pool, jnp.bfloat16))


def unpack_kernel(
    rs, qs, singles, part, one_ref, two_ref, parta_ref, partb_ref, eye_ref, out_ref, power_ref
):
    r, q = (lax.axis_index(name) for name in ("row", "col"))
    half = rs // 2
    step = pl.program_id(0)
    summed = step >= singles

    def turned(value):
        return lax.dot_general(
            eye_ref[...], value, (((1,), (1,)), ((), ())), preferred_element_type=jnp.float32
        )

    def straight_pair(ref, at):
        return ref[0, at].astype(jnp.float32), ref[1, at].astype(jnp.float32)

    def turned_pair(ref, at):
        return turned(ref[0, at]), -turned(ref[1, at])

    def packed_pair(ref, at):
        wide, over = ref[0, at].astype(jnp.float32), turned(ref[0, at])
        return 0.5 * (wide + over), 0.5 * (wide - over)

    def put(when, *ways):
        @pl.when(when)
        def _():
            for at in range(out_ref.shape[1]):
                re, im = ways[0](one_ref, at)
                if len(ways) > 1:
                    more_re, more_im = ways[1](two_ref, at)
                    re, im = re + more_re, im + more_im
                out_ref[0, at] = re
                out_ref[1, at] = im

    single = jnp.logical_not(summed)

    def put_power(ref):
        each = power_ref.shape[0] // ref.shape[0]
        for source in range(ref.shape[0]):
            across = ref[source].T
            for at in range(each):
                power_ref[source * each + at] = across[at * part : (at + 1) * part]

    @pl.when(single)
    def _():
        put_power(parta_ref)

    @pl.when(summed)
    def _():
        put_power(partb_ref)

    off = r != q
    over = mirrored(half, step * rs // singles, r, q)
    put(single & (r == q), packed_pair)
    put(single & over, turned_pair)
    put(single & off & jnp.logical_not(over), straight_pair)
    low = mirrored(half, 0, r, q)
    high = mirrored(half, half, r, q)
    put(summed & (r == q), packed_pair, packed_pair)
    put(summed & low, turned_pair, straight_pair)
    put(summed & high, straight_pair, turned_pair)
    neither = jnp.logical_not(low) & jnp.logical_not(high)
    put(summed & off & neither, straight_pair, straight_pair)


def unpack(block, whole, halved, alone, shared):
    _, rs, qs = sizes()
    cells = rs * qs
    singles = cells * alone // shared
    _, _, height, width = block.shape
    _, beams, lanes = whole.shape
    part = lanes // shared
    steps = singles + cells // 2
    shape = (2, shared, height, width)
    visibility, power = pl.pallas_call(
        functools.partial(unpack_kernel, rs, qs, singles, part),
        grid=(steps,),
        out_shape=(
            jax.ShapeDtypeStruct((2, steps * shared, height, width), jnp.float32),
            jax.ShapeDtypeStruct((steps * shared, part, beams), jnp.float32),
        ),
        in_specs=[
            pl.BlockSpec(shape, lambda i: (0, i, 0, 0)),
            pl.BlockSpec(shape, lambda i: (0, jnp.maximum(i, singles) + cells // 2, 0, 0)),
            pl.BlockSpec((shared // alone, beams, lanes), lambda i: (jnp.minimum(i, singles - 1), 0, 0)),
            pl.BlockSpec((1, beams, lanes), lambda i: (jnp.maximum(i - singles, 0), 0, 0)),
            pl.BlockSpec((height, width), lambda i: (0, 0)),
        ],
        out_specs=(
            pl.BlockSpec(shape, lambda i: (0, i, 0, 0)),
            pl.BlockSpec((shared, part, beams), lambda i: (i, 0, 0)),
        ),
        compiler_params=pltpu.CompilerParams(vmem_limit_bytes=40 << 20),
        name="unpack",
    )(block, block, whole, halved, jnp.asarray(np.eye(height), jnp.bfloat16))
    return visibility, jnp.transpose(power, (0, 2, 1))


def by_channels(voltages, input_flags, channel_order, beam_weights):
    cs, rs, qs = sizes()
    own = NCH // (cs * rs * qs)
    alone, shared, early = own // 2, own, own // 2
    xa, xe, rest = turn(voltages, input_flags, channel_order, alone, shared, early)
    frames = voltages.shape[2] // NCH
    block, whole, halved = products(xa, xe, rest, beam_weights, frames, shared)[:3]
    return unpack(block, whole, halved, alone, shared)


def on_device(voltages, input_flags, channel_order, beam_weights):
    cs, rs, qs = sizes()
    lanes = 2 * (voltages.shape[2] // NCH)
    devices = cs * rs * qs
    square = rs == qs and rs % 2 == 0 and rs > 2 and NCH // devices % 2 == 0
    whole = square and NCH % devices == 0 and lanes % 128 == 0 and voltages.shape[1] % 16 == 0
    if whole and NCH // devices * (lanes // 2 * qs // INTEG) % 128 == 0:
        plan = by_channels
    else:
        plan = by_panels
    return plan(voltages, input_flags, channel_order, beam_weights)


def solution(mesh):
    placed = (P(None, "chan", ("row", "col")), P("chan"), P(), P(None, "chan", "col", None))
    return jax.shard_map(
        on_device,
        mesh=mesh,
        in_specs=placed,
        out_specs=(P(None, "chan", "row", "col"), P("chan", "col", "row")),
        check_vma=False,
    )
```

```python
import functools
import math

import jax
import jax.numpy as jnp
import numpy as np
from jax import lax
from jax.experimental import pallas as pl
from jax.experimental.pallas import tpu as pltpu
from jax.sharding import PartitionSpec as P

NCH = 128
TAPS = 4
INTEG = 8


def passed_along(value, axis, steps):
    count = lax.axis_size(axis)
    initial, last = (max(0, -steps), min(count, count - steps))
    return lax.ppermute(value, axis, [(source, source + steps) for source in range(initial, last)])


def prototype(taps, length):
    position = jnp.arange(taps * length, dtype=jnp.float32) + 0.5
    offset = position / length - taps / 2.0
    window = 0.5 - 0.5 * jnp.cos(2.0 * math.pi * position / (taps * length))
    return (jnp.sin(math.pi * offset) / (math.pi * offset) * window).reshape(taps, length)


def prototype_values(taps, length):
    position = np.arange(taps * length) + 0.5
    offset = position / length - taps / 2.0
    window = 0.5 - 0.5 * np.cos(2.0 * math.pi * position / (taps * length))
    return (np.sin(math.pi * offset) / (math.pi * offset) * window).reshape(taps, length)


def dft_tables(channel_rows, length):
    sample_index = jnp.arange(length, dtype=jnp.int32)
    product = channel_rows[:, None] * sample_index[None, :] % length
    angle = 2.0 * math.pi / length * product.astype(jnp.float32)
    factor = 1.0 / math.sqrt(length)
    cosine = jnp.cos(angle) * factor
    sine = jnp.sin(angle) * factor
    real_rows = jnp.stack([cosine, sine], axis=1)
    imag_rows = jnp.stack([-sine, cosine], axis=1)
    return jnp.stack([real_rows, imag_rows], axis=1).astype(jnp.bfloat16)


def to_frames(gathered, frames, outer, inner, swapped):
    chans = gathered.shape[0]
    width = gathered.shape[1]
    split = gathered.reshape(chans, width, outer, inner, 2, frames)
    if swapped:
        order = jnp.transpose(split, (0, 4, 1, 3, 2, 5))
    else:
        order = jnp.transpose(split, (0, 4, 1, 2, 3, 5))
    return order.reshape(chans, 2, width, outer * inner * frames)


def correlate_one(left_block, right_block, frame_count):
    left_re = left_block[0]
    left_im = left_block[1]
    right_re = right_block[0]
    right_im = right_block[1]
    dims = (((1,), (1,)), ((), ()))
    vis_re = lax.dot_general(left_re, right_re, dims, preferred_element_type=jnp.float32)
    vis_re = vis_re + lax.dot_general(left_im, right_im, dims, preferred_element_type=jnp.float32)
    vis_im = lax.dot_general(left_im, right_re, dims, preferred_element_type=jnp.float32)
    vis_im = vis_im - lax.dot_general(left_re, right_im, dims, preferred_element_type=jnp.float32)
    return jnp.stack([vis_re, vis_im]) / frame_count


def correlate(left_view, right_view, frame_count):
    result = lax.map(
        lambda items: correlate_one(items[0], items[1], frame_count), (left_view, right_view)
    )
    return jnp.transpose(result, (1, 0, 2, 3))


def beams_one(weights, block):
    w_real = weights[0]
    w_imag = weights[1]
    x_real = block[0]
    x_imag = block[1]
    beam_re = jnp.dot(w_real, x_real, preferred_element_type=jnp.float32) - jnp.dot(
        w_imag, x_imag, preferred_element_type=jnp.float32
    )
    beam_im = jnp.dot(w_real, x_imag, preferred_element_type=jnp.float32) + jnp.dot(
        w_imag, x_real, preferred_element_type=jnp.float32
    )
    return jnp.stack([beam_re, beam_im], axis=1)


def form_beams(weights, view):
    by_channel = jnp.transpose(weights, (1, 0, 2, 3))
    return lax.map(lambda items: beams_one(items[0], items[1]), (by_channel, view))


def integrate(voltage):
    power = voltage[:, :, 0] * voltage[:, :, 0] + voltage[:, :, 1] * voltage[:, :, 1]
    return power.reshape(power.shape[0], power.shape[1], -1, INTEG).mean(axis=-1)


def channelize(voltages, input_flags, channel_order):
    masked = voltages * input_flags.astype(jnp.bfloat16)[None, :, None]
    local_inputs = masked.shape[1]
    frames = masked.shape[2] // NCH
    history = passed_along(masked[:, :, masked.shape[2] - (TAPS - 1) * NCH :], ("row", "col"), 1)
    joined = jnp.concatenate([history, masked], axis=2)
    blocks = joined.reshape(2, local_inputs, frames + TAPS - 1, NCH)
    coeffs = prototype(TAPS, NCH)
    filtered = jnp.zeros((2, local_inputs, frames, NCH), jnp.float32)
    for tap_index in range(TAPS):
        filtered = filtered + coeffs[tap_index] * blocks[
            :, :, tap_index : tap_index + frames
        ].astype(jnp.float32)
    filtered = filtered.astype(jnp.bfloat16)
    tables = dft_tables(channel_order, NCH)
    spectrum = jnp.einsum(
        "kqpn,pifn->kiqf",
        tables.astype(jnp.float32),
        filtered.astype(jnp.float32),
        precision=lax.Precision.HIGHEST,
    ).astype(jnp.bfloat16)
    spectrum = spectrum.reshape(NCH, local_inputs, 2 * frames)
    return spectrum


def by_panels(voltages, input_flags, channel_order, beam_weights):
    spectrum = channelize(voltages, input_flags, channel_order)
    frames = spectrum.shape[2] // 2
    turned = lax.all_to_all(spectrum, "chan", split_axis=0, concat_axis=1, tiled=True)
    row_count = lax.axis_size("row")
    col_count = lax.axis_size("col")
    total_frames = frames * row_count * col_count
    row_turned = lax.all_to_all(turned, "row", split_axis=1, concat_axis=2, tiled=True)
    row_all = lax.all_gather(row_turned, "col", axis=2, tiled=True)
    col_turned = lax.all_to_all(turned, "col", split_axis=1, concat_axis=2, tiled=True)
    col_all = lax.all_gather(col_turned, "row", axis=2, tiled=True)
    row_view = to_frames(row_all, frames, col_count, row_count, True)
    col_view = to_frames(col_all, frames, row_count, col_count, False)
    visibility = correlate(row_view, col_view, total_frames)
    weights_all = lax.all_gather(beam_weights, "col", axis=2, tiled=True)
    local_view = to_frames(turned, frames, 1, 1, False)
    voltage = form_beams(weights_all, local_view)
    own_power = integrate(voltage)
    beam_power = lax.all_to_all(own_power, "col", split_axis=1, concat_axis=2, tiled=True)
    return (visibility, beam_power)


MESH = pl.DeviceIdType.MESH


def spectra_tile(v_ref, h_ref, flag_ref, coeff_ref, table_ref, filtered_ref, wide_ref):
    tile = v_ref.shape[1]
    frames = v_ref.shape[2] // NCH
    lanes = 2 * frames
    flag = jnp.broadcast_to(flag_ref[...].astype(jnp.float32), (tile, NCH))
    rows = [jnp.broadcast_to(coeff_ref[tap : tap + 1, :], (tile, NCH)) for tap in range(TAPS)]
    for part in range(2):

        def frame_at(index):
            ref, at = (h_ref, index) if index < TAPS - 1 else (v_ref, index - TAPS + 1)
            return ref[part, :, at * NCH : (at + 1) * NCH].astype(jnp.float32) * flag

        window = [frame_at(index) for index in range(TAPS - 1)]
        for frame in range(frames):
            window = window[-(TAPS - 1) :] + [frame_at(frame + TAPS - 1)]
            total = rows[0] * window[0]
            for tap in range(1, TAPS):
                total = total + rows[tap] * window[tap]
            filtered_ref[part, frame] = total
    for first in range(0, tile, 2):
        stack = []
        for index in (first, first + 1):
            re = filtered_ref[0, :, index, :].astype(jnp.bfloat16)
            im = filtered_ref[1, :, index, :].astype(jnp.bfloat16)
            stack.append(jnp.concatenate([re, im], axis=1))
            stack.append(jnp.concatenate([im, -re], axis=1))
        both = lax.dot_general(
            table_ref[...],
            jnp.concatenate(stack, axis=0),
            (((1,), (1,)), ((), ())),
            preferred_element_type=jnp.float32,
        )
        wide_ref[:, first, :] = both[:, :lanes]
        wide_ref[:, first + 1, :] = both[:, lanes:]
    return wide_ref[...].astype(jnp.bfloat16)


def sizes():
    return lax.axis_size("chan"), lax.axis_size("row"), lax.axis_size("col")


def part_of(c, r, q, cs, half, qs, step):
    inner = step // cs
    row = r // half * half + (r % half + inner % half) % half
    return (c + step % cs) % cs, row, (q + inner // half) % qs


def turn_kernel(
    cs, rs, qs, tile, group, wide, alone, early,
    v_ref, flag_ref, coeff_ref, table_ref, whole_ref, x_ref, e_ref, s_ref,
    filtered_ref, wide_ref, spec_ref, past_ref, send, recv, psend, precv, local,
):
    c, r, q = (lax.axis_index(name) for name in ("chan", "row", "col"))
    half = rs // 2
    cells = rs * qs
    halves = half * qs
    devices = cs * cells
    me = r * qs + q
    mine = me % halves
    here = c * cells + me
    inputs = spec_ref.shape[1]
    lanes = spec_ref.shape[2]
    early_base = devices * alone
    late_base = early_base + cs * halves * early
    turn_step = pl.program_id(0)
    tiles = inputs // tile

    def ahead(step):
        return (r + step % rs) % rs * qs + (q + step // rs) % qs

    def rows_at(first, count):
        return pl.ds(pl.multiple_of(first, tile), count)

    def spectra(step, first, count):
        chan, cell = (c + step % cs) % cs, ahead(step // cs)
        origin, column = c, me
        return pltpu.make_async_remote_copy(
            src_ref=spec_ref.at[
                pl.ds((chan * cells + cell) * alone, alone), rows_at(first, count)
            ],
            dst_ref=x_ref.at[
                :,
                rows_at(origin * inputs + first, count),
                pl.ds(pl.multiple_of(column * lanes, lanes), lanes),
            ],
            send_sem=send.at[0],
            recv_sem=recv.at[0],
            device_id=(chan, cell // qs, cell % qs),
            device_id_type=MESH,
        )

    def sooner(step, first, count):
        chan, row, col = part_of(c, r, q, cs, half, qs, step)
        place = row % half * qs + col
        origin, column = c, mine
        return pltpu.make_async_remote_copy(
            src_ref=spec_ref.at[
                pl.ds(early_base + (chan * halves + place) * early, early), rows_at(first, count)
            ],
            dst_ref=e_ref.at[
                :,
                rows_at(origin * inputs + first, count),
                pl.ds(pl.multiple_of(column * lanes, lanes), lanes),
            ],
            send_sem=send.at[1],
            recv_sem=recv.at[1],
            device_id=(chan, row, col),
            device_id_type=MESH,
        )

    past = past_ref.shape[2]
    chunk = tile if inputs % wide else wide

    def last_frames(first):
        following = (me + 1) % cells
        rows = rows_at(first, chunk)
        return pltpu.make_async_remote_copy(
            src_ref=whole_ref.at[:, rows, pl.ds(whole_ref.shape[2] - past, past)],
            dst_ref=past_ref.at[:, rows],
            send_sem=psend.at[0],
            recv_sem=precv.at[first // chunk],
            device_id=(c, following // qs, following % qs),
            device_id_type=MESH,
        )

    @pl.when((turn_step == 0) & (me + 1 < cells))
    def _():
        for first in range(0, inputs, chunk):
            last_frames(first).start()

    @pl.when((turn_step == 0) & (me == 0))
    def _():
        past_ref[...] = jnp.zeros_like(past_ref)

    @pl.when((turn_step < tiles) & (me > 0) & (turn_step * tile % chunk == 0))
    def _():
        last_frames(turn_step * tile).wait_recv()

    @pl.when((turn_step == tiles) & (me + 1 < cells))
    def _():
        pltpu.make_async_remote_copy(
            src_ref=past_ref,
            dst_ref=past_ref,
            send_sem=psend.at[0],
            recv_sem=precv.at[0],
            device_id=(c, r, q),
            device_id_type=MESH,
        ).wait_send()

    @pl.when((turn_step > 0) & (turn_step * tile % group == 0))
    def _():
        def start(step, carry):
            spectra(step, turn_step * tile - group, group).start()
            return carry

        lax.fori_loop(1, devices, start, 0)

    @pl.when((turn_step > 0) & (turn_step * tile % wide == 0))
    def _():
        def start(step, carry):
            sooner(step, turn_step * tile - wide, wide).start()
            return carry

        lax.fori_loop(1, cs * halves, start, 0)

    @pl.when(turn_step < tiles)
    def _():
        at = pl.ds(pl.multiple_of(turn_step * tile, tile), tile)
        spec_ref[:, at, :] = spectra_tile(
            v_ref, past_ref.at[:, at], flag_ref, coeff_ref, table_ref, filtered_ref, wide_ref
        )

    @pl.when(turn_step == tiles)
    def _():
        stays = [
            pltpu.make_async_copy(
                spec_ref.at[pl.ds(here * alone, alone)],
                x_ref.at[
                    :, rows_at(c * inputs, inputs), pl.ds(pl.multiple_of(me * lanes, lanes), lanes)
                ],
                local.at[0],
            ),
            pltpu.make_async_copy(
                spec_ref.at[pl.ds(early_base + (c * halves + mine) * early, early)],
                e_ref.at[
                    :,
                    rows_at(c * inputs, inputs),
                    pl.ds(pl.multiple_of(mine * lanes, lanes), lanes),
                ],
                local.at[1],
            ),
            pltpu.make_async_copy(
                spec_ref.at[pl.ds(late_base, s_ref.shape[0])], s_ref, local.at[2]
            ),
        ]
        for stay in stays:
            stay.start()

        for index, count in enumerate(((devices - 1) * alone, (cs * halves - 1) * early)):
            rows = spec_ref.at[pl.ds(0, count)]
            every = pltpu.make_async_remote_copy(
                src_ref=rows,
                dst_ref=rows,
                send_sem=send.at[index],
                recv_sem=recv.at[index],
                device_id=(c, r, q),
                device_id_type=MESH,
            )
            every.wait_send()
            every.wait_recv()
        for stay in stays:
            stay.wait()


def turn(voltages, input_flags, channel_order, alone, shared, early):
    cs, rs, qs = sizes()
    devices = cs * rs * qs
    halves = rs // 2 * qs
    _, inputs, samples = voltages.shape
    past = (TAPS - 1) * NCH
    frames = samples // NCH
    lanes = 2 * frames
    tile = 16
    group = 2 * tile if inputs % (2 * tile) == 0 else tile
    wide = 4 * group if inputs % (4 * group) == 0 else group
    last = inputs // tile - 1
    place = channel_order.reshape(cs, NCH // cs)
    split = place[:, rs * qs * alone :].reshape(cs, halves, shared)
    order = jnp.concatenate(
        [
            place[:, : rs * qs * alone].reshape(-1),
            split[:, :, :early].reshape(-1),
            split[:, :, early:].reshape(-1),
        ]
    )
    tables = dft_tables(order, NCH)[:, 0].reshape(NCH, 2 * NCH)
    anywhere = pl.BlockSpec(memory_space=pl.ANY)
    counts = (2, 2, 1, inputs // tile, 3)
    return pl.pallas_call(
        functools.partial(turn_kernel, cs, rs, qs, tile, group, wide, alone, early),
        grid=(inputs // tile + 1,),
        out_shape=(
            jax.ShapeDtypeStruct((alone, inputs * cs, lanes * rs * qs), jnp.bfloat16),
            jax.ShapeDtypeStruct((early, inputs * cs, lanes * halves), jnp.bfloat16),
            jax.ShapeDtypeStruct((cs * halves * (shared - early), inputs, lanes), jnp.bfloat16),
        ),
        in_specs=[
            pl.BlockSpec((2, tile, samples), lambda i: (0, jnp.minimum(i, last), 0)),
            pl.BlockSpec((tile, 1), lambda i: (jnp.minimum(i, last), 0)),
            pl.BlockSpec((TAPS, NCH), lambda i: (0, 0)),
            pl.BlockSpec((NCH, 2 * NCH), lambda i: (0, 0)),
            anywhere,
        ],
        out_specs=(anywhere,) * 3,
        scratch_shapes=[
            pltpu.VMEM((2, frames, tile, NCH), jnp.float32),
            pltpu.VMEM((NCH, tile, lanes), jnp.float32),
            pltpu.VMEM((NCH, inputs, lanes), jnp.bfloat16),
            pltpu.VMEM((2, inputs, past), jnp.bfloat16),
        ]
        + [pltpu.SemaphoreType.DMA((count,)) for count in counts],
        compiler_params=pltpu.CompilerParams(has_side_effects=True, vmem_limit_bytes=60 << 20),
        name="turn",
    )(
        voltages,
        input_flags[:, None],
        jnp.asarray(prototype_values(TAPS, NCH), jnp.float32),
        tables,
        voltages,
    )


def crosses(half, source_row, row, col):
    return (row != col) & (row // half == col // half) & (source_row // half != row // half)


def nearer(half, row, col):
    upper = row // half == 1
    return (upper & (row < col)) | (jnp.logical_not(upper) & (row > col))


def mirrored(half, source_row, row, col):
    return crosses(half, source_row, row, col) & jnp.logical_not(nearer(half, row, col))


def products_kernel(
    cs, rs, qs, frame_count, alone, early,
    xa_ref, xe_ref, s_ref, weight_ref, swap_ref, pool_ref,
    block_ref, parta_ref, partb_ref, late_ref, all_ref, stage_ref,
    x_ref, y_ref, w_ref, vis_ref, powera_ref, powerb_ref,
    load, send, recv, stage_send, stage_recv, relay_send,
    psend, precv, lsend, lrecv, wsend, wrecv, wload, local,
):
    c, r, q = (lax.axis_index(name) for name in ("chan", "row", "col"))
    cells = rs * qs
    half = rs // 2
    halves = half * qs
    me = r * qs + q
    mine = me % halves
    held, inputs = vis_ref.shape[1], vis_ref.shape[2]
    shared = held - alone
    late = shared - early
    depth = x_ref.shape[2]
    depths = {False: depth, True: depth // 2}
    lanes = swap_ref.shape[0]
    own_inputs = inputs // cs
    height, width = block_ref.shape[2], block_ref.shape[3]
    part_height, part_width = parta_ref.shape[1], parta_ref.shape[2]
    now = pl.program_id(0)

    def ahead(step, sign):
        row = (r + rs + sign * (step % rs)) % rs
        return row * qs + (q + qs + sign * (step // rs)) % qs

    def vis_at(planes, first, count, row, col):
        return vis_ref.at[
            pl.ds(0, planes),
            pl.ds(first, count),
            pl.ds(pl.multiple_of(row * height, height), height),
            pl.ds(pl.multiple_of(col * width, width), width),
        ]

    def power_at(ref, row, col):
        return ref.at[
            pl.ds(pl.multiple_of(col * part_height, part_height), part_height),
            pl.ds(pl.multiple_of(row * part_width, part_width), part_width),
        ]

    def landing(kind, planes, cell, first, count):
        base = cells * alone + cell * shared if kind else cell * alone
        return block_ref.at[pl.ds(0, planes), pl.ds(base + first, count)]

    def outgoing(kind, planes, cell, first, count):
        return pltpu.make_async_remote_copy(
            src_ref=vis_at(planes, first + (alone if kind else 0), count, cell // qs, cell % qs),
            dst_ref=landing(kind, planes, me, first, count),
            send_sem=send.at[planes - 1],
            recv_sem=recv.at[0],
            device_id=(c, cell // qs, cell % qs),
            device_id_type=MESH,
        )

    def together(rows, leaves, comes):
        return pltpu.make_async_remote_copy(
            src_ref=rows,
            dst_ref=rows,
            send_sem=leaves,
            recv_sem=comes,
            device_id=(c, r, q),
            device_id_type=MESH,
        )

    def staged(pair, row, first, count):
        return stage_ref.at[:, pl.ds((pair * half + row % half) * held + first, count)]

    def to_relay(row, col, first, count):
        inner = jnp.where(r < half, row - half, half - 1 - row)
        outer = jnp.where(r < half, col - half, half - 1 - col)
        pair = inner * (2 * half - inner - 1) // 2 + outer - inner - 1
        return pltpu.make_async_remote_copy(
            src_ref=vis_at(2, first, count, row, col),
            dst_ref=staged(pair, r, first, count),
            send_sem=stage_send.at[0],
            recv_sem=stage_recv.at[(pair * half + r % half) * held + first],
            device_id=(c, jnp.where(r < half, half, half - 1), q),
            device_id_type=MESH,
        )

    def at_relay(pair, row, first):
        return pltpu.make_async_remote_copy(
            src_ref=staged(pair, row, first, 1),
            dst_ref=staged(pair, row, first, 1),
            send_sem=stage_send.at[0],
            recv_sem=stage_recv.at[(pair * half + row % half) * held + first],
            device_id=(c, row, q),
            device_id_type=MESH,
        )

    def from_relay(kind, pair, row, at, first, count, goal):
        return pltpu.make_async_remote_copy(
            src_ref=staged(pair, row, first, count),
            dst_ref=landing(kind, 2, row * qs + q, at, count),
            send_sem=relay_send.at[0],
            recv_sem=recv.at[0],
            device_id=(c,) + goal,
            device_id_type=MESH,
        )

    relays = r == jnp.where(r < half, half - 1, half)
    pairs = [(inner, outer) for inner in range(half) for outer in range(inner + 1, half)]

    def owners(pair):
        inner, outer = pairs[pair]
        row = jnp.where(r < half, half - 1 - inner, half + inner)
        col = jnp.where(r < half, half - 1 - outer, half + outer)
        return row, col

    def both(diagonal, sent, act):
        @pl.when(sent & diagonal)
        def _():
            act(1)

        @pl.when(sent & jnp.logical_not(diagonal))
        def _():
            act(2)

    def part(kind, cell, slot):
        source, goal = (powerb_ref, partb_ref) if kind else (powera_ref, parta_ref)
        row = cell // qs % half if kind else cell // qs
        place = slot % halves if kind else slot
        return pltpu.make_async_remote_copy(
            src_ref=power_at(source, row, cell % qs),
            dst_ref=goal.at[place],
            send_sem=psend.at[1 if kind else 0],
            recv_sem=precv.at[1 if kind else 0],
            device_id=(c, cell // qs, cell % qs),
            device_id_type=MESH,
        )

    peers = cs * halves

    def spread(step, at):
        chan, row, col = part_of(c, r, q, cs, half, qs, step)
        place = row % half * qs + col
        origin, column = c, mine
        return pltpu.make_async_remote_copy(
            src_ref=s_ref.at[(chan * halves + place) * late + at],
            dst_ref=late_ref.at[
                at,
                pl.ds(pl.multiple_of(origin * own_inputs, own_inputs), own_inputs),
                pl.ds(pl.multiple_of(column * lanes, lanes), lanes),
            ],
            send_sem=lsend.at[0],
            recv_sem=lrecv.at[at],
            device_id=(chan, row, col),
            device_id_type=MESH,
        )

    def stay_late(at):
        return pltpu.make_async_copy(
            s_ref.at[(c * halves + mine) * late + at],
            late_ref.at[
                at,
                pl.ds(pl.multiple_of(c * own_inputs, own_inputs), own_inputs),
                pl.ds(pl.multiple_of(mine * lanes, lanes), lanes),
            ],
            local.at[4],
        )

    def fetch(source, slot, kind):
        return pltpu.make_async_copy(
            source, x_ref.at[slot, :, pl.ds(0, depths[kind])], load.at[slot]
        )

    def weight_spans(peer):
        cell = r * qs + peer
        return (
            (cell * alone, 0, alone),
            (cells * alone + cell % halves * shared, alone, shared),
        )

    def weights_at(slot, goal, count):
        beams = weight_ref.shape[2]
        return all_ref.at[
            :, pl.ds(goal, count), pl.ds(pl.multiple_of(slot * beams, beams), beams)
        ]

    def weights(peer, slot, source, goal, count):
        return pltpu.make_async_remote_copy(
            src_ref=weight_ref.at[:, pl.ds(source, count)],
            dst_ref=weights_at(slot, goal, count),
            send_sem=wsend.at[peer],
            recv_sem=wrecv.at[slot],
            device_id=(c, r, peer),
            device_id_type=MESH,
        )

    keeps = [
        pltpu.make_async_copy(
            weight_ref.at[:, pl.ds(source, count)], weights_at(q, goal, count), local.at[5 + index]
        )
        for index, (source, goal, count) in enumerate(weight_spans(q))
    ]

    def fetch_weights(index, slot):
        return pltpu.make_async_copy(all_ref.at[:, index], w_ref.at[slot], wload.at[slot])

    def visibility_of(kind, slot, at):
        deep = depths[kind]
        across = (((1,), (1,)), ((), ()))
        index = at + (alone if kind else 0)

        def panels(step, carry):
            col = (q + step) % qs
            span = pl.ds(pl.multiple_of(col * width, width), width)
            for start in range(0, deep, lanes):
                y_ref[:, start : start + lanes] = jnp.dot(
                    x_ref[slot, span, start : start + lanes],
                    swap_ref[...],
                    preferred_element_type=jnp.float32,
                ).astype(jnp.bfloat16)
            every = x_ref[slot, :, :deep]
            re = lax.dot_general(
                every, x_ref[slot, span, :deep], across, preferred_element_type=jnp.float32
            )
            im = lax.dot_general(every, y_ref[:, :deep], across, preferred_element_type=jnp.float32)
            panel = lax.broadcasted_iota(jnp.int32, re.shape, 0) // height
            first = jnp.where(panel == col, re + im, re)
            vis_ref[0, index, :, span] = (first / frame_count).astype(vis_ref.dtype)
            vis_ref[1, index, :, span] = (im / frame_count).astype(vis_ref.dtype)

            def start(step, carry):
                outward = jnp.where(step % 2 == 0, half + step // 2, half - 1 - step // 2)
                row = jnp.where(r < half, outward, rs - 1 - outward)
                cell = row * qs + col
                shared_pair = crosses(half, r, row, col)
                sent = (cell != me) & jnp.logical_not(shared_pair)
                both(row == col, sent, lambda planes: outgoing(kind, planes, cell, at, 1).start())

                @pl.when(shared_pair & nearer(half, row, col))
                def _():
                    to_relay(row, col, index, 1).start()

                return carry

            lax.fori_loop(0, rs, start, 0)
            return carry

        lax.fori_loop(0, qs, panels, 0)

    def beams_of(kind, slot, at):
        deep = depths[kind]
        span = 4 * lanes if deep % (4 * lanes) == 0 else lanes
        power_ref = powerb_ref if kind else powera_ref
        columns_out = power_ref.shape[1]
        middle = lanes // 2

        def columns(step, carry):
            along = pl.ds(pl.multiple_of(step * span, span), span)
            x = x_ref[slot, :, along]
            straight = jnp.dot(w_ref[slot, 0], x, preferred_element_type=jnp.float32)
            crossed = jnp.dot(w_ref[slot, 1], x, preferred_element_type=jnp.float32)
            swapped = []
            for start in range(0, span, lanes):
                swapped.append(crossed[:, start + middle : start + lanes])
                swapped.append(-crossed[:, start : start + middle])
            beam = straight - jnp.concatenate(swapped, axis=1)
            square = beam * beam
            high = square.astype(jnp.bfloat16)
            low = (square - high.astype(jnp.float32)).astype(jnp.bfloat16)
            pool = pool_ref[along, :columns_out]
            return (
                carry
                + jnp.dot(high, pool, preferred_element_type=jnp.float32)
                + jnp.dot(low, pool, preferred_element_type=jnp.float32)
            )

        found = lax.fori_loop(0, deep // span, columns, jnp.zeros(power_ref.shape, jnp.float32))
        lane = lax.broadcasted_iota(jnp.int32, power_ref.shape, 1) % part_width
        kept = power_ref[...].astype(jnp.float32)
        kept = jnp.where(lane // (part_width // shared) == at, found, kept)
        power_ref[...] = kept.astype(power_ref.dtype)

    def pass_on(kind, at):
        index = at + (alone if kind else 0)

        @pl.when(relays)
        def _():
            for pair in range(len(pairs)):
                row, col = owners(pair)

                def one(step, carry, pair=pair, row=row, col=col):
                    source = (1 - r // half) * half + step
                    at_relay(pair, source, index).wait_recv()
                    from_relay(kind, pair, source, at, index, 1, (col, row)).start()
                    mine_too = (row == r) & (col == q)

                    @pl.when(mine_too)
                    def _():
                        pltpu.make_async_copy(
                            staged(pair, source, index, 1),
                            landing(kind, 2, source * qs + q, at, 1),
                            recv.at[0],
                        ).start()

                    @pl.when(jnp.logical_not(mine_too))
                    def _():
                        from_relay(kind, pair, source, at, index, 1, (row, col)).start()

                    return carry

                lax.fori_loop(0, half, one, 0)

    locals_ = [
        pltpu.make_async_copy(
            vis_at(2, 0, alone, r, q), landing(False, 2, me, 0, alone), local.at[0]
        ),
        pltpu.make_async_copy(
            vis_at(2, alone, shared, r, q), landing(True, 2, me, 0, shared), local.at[1]
        ),
        pltpu.make_async_copy(power_at(powera_ref, r, q), parta_ref.at[me], local.at[2]),
        pltpu.make_async_copy(power_at(powerb_ref, r % half, q), partb_ref.at[mine], local.at[3]),
    ]
    coming = (now + 1) % held
    next_slot = (now + 1) % 2
    more = now + 1 < 2 * held
    turn_index = now % held

    @pl.when(now == 0)
    def _():
        powera_ref[...] = jnp.zeros_like(powera_ref)
        powerb_ref[...] = jnp.zeros_like(powerb_ref)
        fetch(xa_ref.at[0], 0, False).start()

    @pl.when(now < late)
    def _():
        def start(step, carry):
            spread(step, now).start()
            return carry

        lax.fori_loop(1, cs * halves, start, 0)
        stay = stay_late(now)
        stay.start()
        stay.wait()

    @pl.when(now == late)
    def _():
        def start(step, carry):
            peer = (q + step) % qs
            for source, goal, count in weight_spans(peer):
                weights(peer, q, source, goal, count).start()
            return carry

        lax.fori_loop(1, qs, start, 0)
        for keep in keeps:
            keep.start()

    @pl.when(more & (coming < alone))
    def _():
        fetch(xa_ref.at[coming], next_slot, False).start()

    @pl.when(more & (coming >= alone) & (coming < alone + early))
    def _():
        fetch(xe_ref.at[coming - alone], next_slot, True).start()

    @pl.when(now == held)
    def _():
        def arrive(step, carry):
            behind = (q + qs - step) % qs
            weights(behind, behind, 0, 0, held).wait_recv()
            return carry

        lax.fori_loop(1, qs, arrive, 0)
        for keep in keeps:
            keep.wait()
        fetch_weights(0, held % 2).start()

    @pl.when((now >= held) & more)
    def _():
        fetch_weights(coming, next_slot).start()

    @pl.when((now < 2 * held) & (turn_index < alone))
    def _():
        fetch(xa_ref.at[0], now % 2, False).wait()

        @pl.when(now < held)
        def _():
            visibility_of(False, now % 2, turn_index)

        @pl.when(now >= held)
        def _():
            fetch_weights(0, now % 2).wait()
            beams_of(False, now % 2, turn_index)
            pass_on(False, turn_index)

    @pl.when((now < 2 * held) & (turn_index >= alone))
    def _():
        fetch(xe_ref.at[0], now % 2, True).wait()

        @pl.when(now < held)
        def _():
            visibility_of(True, now % 2, turn_index - alone)

        @pl.when(now >= held)
        def _():
            fetch_weights(0, now % 2).wait()
            beams_of(True, now % 2, turn_index - alone)

        @pl.when(now == 2 * held - 1)
        def _():
            def start(step, carry):
                cell = ahead(step, 1)
                part(False, cell, me).start()

                @pl.when(cell // halves == r // half)
                def _():
                    part(True, cell, me).start()

                return carry

            lax.fori_loop(1, cells, start, 0)
            for copy in locals_:
                copy.start()

        @pl.when(now >= held)
        def _():
            pass_on(True, turn_index - alone)

    @pl.when(more & (coming >= alone + early))
    def _():
        at = coming - alone - early

        @pl.when(now < held)
        def _():
            together(s_ref.at[pl.ds(0, peers - 1)], lsend.at[0], lrecv.at[at]).wait_recv()

        fetch(late_ref.at[at], next_slot, True).start()

    @pl.when(now == 2 * held)
    def _():
        plain = cells - 1 - rs - 2 * len(pairs)

        def sent(diagonal, straight):
            for planes, count in ((1, diagonal), (2, straight)):
                rows = block_ref.at[pl.ds(0, planes), pl.ds(0, count * held)]
                together(rows, send.at[planes - 1], recv.at[0]).wait_send()

        @pl.when(r == q)
        def _():
            sent(rs - 1, plain + 1)
            rows = block_ref.at[pl.ds(0, 1), pl.ds(0, (cells - 1) * held)]
            together(rows, send.at[0], recv.at[0]).wait_recv()

        @pl.when(r != q)
        def _():
            sent(rs, plain)
            rows = block_ref.at[pl.ds(0, 2), pl.ds(0, (cells - 1) * held)]
            together(rows, send.at[0], recv.at[0]).wait_recv()

        rows = block_ref.at[pl.ds(0, 2), pl.ds(0, len(pairs) * held)]
        together(rows, stage_send.at[0], recv.at[0]).wait_send()
        for index, (ref, count) in enumerate(((parta_ref, cells - 1), (partb_ref, halves - 1))):
            every = together(ref.at[pl.ds(0, count)], psend.at[index], precv.at[index])
            every.wait_send()
            every.wait_recv()

        @pl.when(relays)
        def _():
            own = jnp.where(r < half, r > q, r < q) & (r // half == q // half)
            all_passed = 2 * len(pairs) * half * held

            def passed(count):
                rows = block_ref.at[pl.ds(0, 2), pl.ds(0, count)]
                together(rows, relay_send.at[0], recv.at[0]).wait_send()

            @pl.when(own)
            def _():
                passed(all_passed - half * held)

            @pl.when(jnp.logical_not(own))
            def _():
                passed(all_passed)

        together(s_ref.at[pl.ds(0, late * (peers - 1))], lsend.at[0], lrecv.at[0]).wait_send()

        def sent_weights(step, carry):
            weights((q + step) % qs, q, 0, 0, held).wait_send()
            return carry

        lax.fori_loop(1, qs, sent_weights, 0)
        for copy in locals_:
            copy.wait()


def products(xa, xe, rest, weights, frames, shared):
    cs, rs, qs = sizes()
    cells = rs * qs
    halves = cells // 2
    alone, inputs, depth = xa.shape
    early = xe.shape[0]
    late = shared - early
    held = alone + shared
    beams = weights.shape[2] * qs
    bins = depth // (2 * INTEG)
    lanes = 2 * frames
    source = np.arange(lanes)[:, None]
    goal = np.arange(lanes)[None, :]
    swap = np.where(source + frames == goal, 1.0, 0.0) - np.where(source == goal + frames, 1.0, 0.0)
    at = np.arange(depth)
    frame = at // lanes * frames + at % frames
    part = bins // rs
    column = np.arange(rs * shared * part)
    bin_of = column // (shared * part) * part + column % part
    pool = np.where(frame[:, None] // INTEG == bin_of[None, :], 1.0 / INTEG, 0.0)
    anywhere = pl.BlockSpec(memory_space=pl.ANY)
    half = rs // 2
    pairs = half * (half - 1) // 2
    stages = pairs * half * held
    counts = (2, 2, 1, 1, stages, 1, 2, 2, 1, late, qs, qs, 2, 7)
    return pl.pallas_call(
        functools.partial(products_kernel, cs, rs, qs, depth // 2, alone, early),
        grid=(2 * held + 1,),
        out_shape=(
            jax.ShapeDtypeStruct((2, cells * held, inputs // rs, inputs // qs), jnp.bfloat16),
            jax.ShapeDtypeStruct((cells, beams // qs, shared * part), jnp.bfloat16),
            jax.ShapeDtypeStruct((halves, beams // qs, shared * part), jnp.bfloat16),
            jax.ShapeDtypeStruct((late, inputs, depth // 2), jnp.bfloat16),
            jax.ShapeDtypeStruct((2, held, beams, inputs), weights.dtype),
            jax.ShapeDtypeStruct((2, stages, inputs // rs, inputs // qs), jnp.bfloat16),
        ),
        in_specs=[
            anywhere,
            anywhere,
            anywhere,
            anywhere,
            pl.BlockSpec((lanes, lanes), lambda j: (0, 0)),
            pl.BlockSpec((depth, rs * shared * part), lambda j: (0, 0)),
        ],
        out_specs=(anywhere,) * 6,
        scratch_shapes=[
            pltpu.VMEM((2, inputs, depth), jnp.bfloat16),
            pltpu.VMEM((inputs // qs, depth), jnp.bfloat16),
            pltpu.VMEM((2, 2, beams, inputs), weights.dtype),
            pltpu.VMEM((2, held, inputs, inputs), jnp.bfloat16),
            pltpu.VMEM((beams, rs * shared * part), jnp.bfloat16),
            pltpu.VMEM((beams, rs // 2 * shared * part), jnp.bfloat16),
        ]
        + [pltpu.SemaphoreType.DMA((count,)) for count in counts],
        compiler_params=pltpu.CompilerParams(has_side_effects=True, vmem_limit_bytes=60 << 20),
        name="products",
    )(xa, xe, rest, weights, jnp.asarray(swap, jnp.bfloat16), jnp.asarray(pool, jnp.bfloat16))


def unpack_kernel(
    rs, qs, singles, part, one_ref, two_ref, parta_ref, partb_ref, eye_ref, out_ref, power_ref
):
    r, q = (lax.axis_index(name) for name in ("row", "col"))
    half = rs // 2
    step = pl.program_id(0)
    summed = step >= singles

    def turned(value):
        return lax.dot_general(
            eye_ref[...], value, (((1,), (1,)), ((), ())), preferred_element_type=jnp.float32
        )

    def straight_pair(ref, at):
        return ref[0, at].astype(jnp.float32), ref[1, at].astype(jnp.float32)

    def turned_pair(ref, at):
        return turned(ref[0, at]), -turned(ref[1, at])

    def packed_pair(ref, at):
        wide, over = ref[0, at].astype(jnp.float32), turned(ref[0, at])
        return 0.5 * (wide + over), 0.5 * (wide - over)

    def put(when, *ways):
        @pl.when(when)
        def _():
            for at in range(out_ref.shape[1]):
                re, im = ways[0](one_ref, at)
                if len(ways) > 1:
                    more_re, more_im = ways[1](two_ref, at)
                    re, im = re + more_re, im + more_im
                out_ref[0, at] = re
                out_ref[1, at] = im

    single = jnp.logical_not(summed)

    def put_power(ref):
        each = power_ref.shape[0] // ref.shape[0]
        for source in range(ref.shape[0]):
            across = ref[source].astype(jnp.float32).T
            for at in range(each):
                power_ref[source * each + at] = across[at * part : (at + 1) * part]

    @pl.when(single)
    def _():
        put_power(parta_ref)

    @pl.when(summed)
    def _():
        put_power(partb_ref)

    off = r != q
    over = mirrored(half, step * rs // singles, r, q)
    put(single & (r == q), packed_pair)
    put(single & over, turned_pair)
    put(single & off & jnp.logical_not(over), straight_pair)
    low = mirrored(half, 0, r, q)
    high = mirrored(half, half, r, q)
    put(summed & (r == q), packed_pair, packed_pair)
    put(summed & low, turned_pair, straight_pair)
    put(summed & high, straight_pair, turned_pair)
    neither = jnp.logical_not(low) & jnp.logical_not(high)
    put(summed & off & neither, straight_pair, straight_pair)


def unpack(block, whole, halved, alone, shared):
    _, rs, qs = sizes()
    cells = rs * qs
    singles = cells * alone // shared
    _, _, height, width = block.shape
    _, beams, lanes = whole.shape
    part = lanes // shared
    steps = singles + cells // 2
    shape = (2, shared, height, width)
    visibility, power = pl.pallas_call(
        functools.partial(unpack_kernel, rs, qs, singles, part),
        grid=(steps,),
        out_shape=(
            jax.ShapeDtypeStruct((2, steps * shared, height, width), jnp.float32),
            jax.ShapeDtypeStruct((steps * shared, part, beams), jnp.float32),
        ),
        in_specs=[
            pl.BlockSpec(shape, lambda i: (0, i, 0, 0)),
            pl.BlockSpec(shape, lambda i: (0, jnp.maximum(i, singles) + cells // 2, 0, 0)),
            pl.BlockSpec((shared // alone, beams, lanes), lambda i: (jnp.minimum(i, singles - 1), 0, 0)),
            pl.BlockSpec((1, beams, lanes), lambda i: (jnp.maximum(i - singles, 0), 0, 0)),
            pl.BlockSpec((height, width), lambda i: (0, 0)),
        ],
        out_specs=(
            pl.BlockSpec(shape, lambda i: (0, i, 0, 0)),
            pl.BlockSpec((shared, part, beams), lambda i: (i, 0, 0)),
        ),
        compiler_params=pltpu.CompilerParams(vmem_limit_bytes=60 << 20),
        name="unpack",
    )(block, block, whole, halved, jnp.asarray(np.eye(height), jnp.bfloat16))
    return visibility, jnp.transpose(power, (0, 2, 1))


def by_channels(voltages, input_flags, channel_order, beam_weights):
    cs, rs, qs = sizes()
    own = NCH // (cs * rs * qs)
    alone, shared, early = own // 2, own, own // 2
    xa, xe, rest = turn(voltages, input_flags, channel_order, alone, shared, early)
    frames = voltages.shape[2] // NCH
    block, whole, halved = products(xa, xe, rest, beam_weights, frames, shared)[:3]
    return unpack(block, whole, halved, alone, shared)


def on_device(voltages, input_flags, channel_order, beam_weights):
    cs, rs, qs = sizes()
    lanes = 2 * (voltages.shape[2] // NCH)
    devices = cs * rs * qs
    square = rs == qs and rs % 2 == 0 and rs > 2 and NCH // devices % 2 == 0
    whole = square and NCH % devices == 0 and lanes % 128 == 0 and voltages.shape[1] % 16 == 0
    if whole and NCH // devices * (lanes // 2 * qs // INTEG) % 128 == 0:
        plan = by_channels
    else:
        plan = by_panels
    return plan(voltages, input_flags, channel_order, beam_weights)


def solution(mesh):
    placed = (P(None, "chan", ("row", "col")), P("chan"), P(), P(None, "chan", "col", None))
    return jax.shard_map(
        on_device,
        mesh=mesh,
        in_specs=placed,
        out_specs=(P(None, "chan", "row", "col"), P("chan", "col", "row")),
        check_vma=False,
    )
```

```python
import functools
import math

import jax
import jax.numpy as jnp
import numpy as np
from jax import lax
from jax.experimental import pallas as pl
from jax.experimental.pallas import tpu as pltpu
from jax.sharding import PartitionSpec as P

NCH = 128
TAPS = 4
INTEG = 8


def passed_along(value, axis, steps):
    count = lax.axis_size(axis)
    initial, last = (max(0, -steps), min(count, count - steps))
    return lax.ppermute(value, axis, [(source, source + steps) for source in range(initial, last)])


def prototype(taps, length):
    position = jnp.arange(taps * length, dtype=jnp.float32) + 0.5
    offset = position / length - taps / 2.0
    window = 0.5 - 0.5 * jnp.cos(2.0 * math.pi * position / (taps * length))
    return (jnp.sin(math.pi * offset) / (math.pi * offset) * window).reshape(taps, length)


def prototype_values(taps, length):
    position = np.arange(taps * length) + 0.5
    offset = position / length - taps / 2.0
    window = 0.5 - 0.5 * np.cos(2.0 * math.pi * position / (taps * length))
    return (np.sin(math.pi * offset) / (math.pi * offset) * window).reshape(taps, length)


def dft_tables(channel_rows, length):
    sample_index = jnp.arange(length, dtype=jnp.int32)
    product = channel_rows[:, None] * sample_index[None, :] % length
    angle = 2.0 * math.pi / length * product.astype(jnp.float32)
    factor = 1.0 / math.sqrt(length)
    cosine = jnp.cos(angle) * factor
    sine = jnp.sin(angle) * factor
    real_rows = jnp.stack([cosine, sine], axis=1)
    imag_rows = jnp.stack([-sine, cosine], axis=1)
    return jnp.stack([real_rows, imag_rows], axis=1).astype(jnp.bfloat16)


def to_frames(gathered, frames, outer, inner, swapped):
    chans = gathered.shape[0]
    width = gathered.shape[1]
    split = gathered.reshape(chans, width, outer, inner, 2, frames)
    if swapped:
        order = jnp.transpose(split, (0, 4, 1, 3, 2, 5))
    else:
        order = jnp.transpose(split, (0, 4, 1, 2, 3, 5))
    return order.reshape(chans, 2, width, outer * inner * frames)


def correlate_one(left_block, right_block, frame_count):
    left_re = left_block[0]
    left_im = left_block[1]
    right_re = right_block[0]
    right_im = right_block[1]
    dims = (((1,), (1,)), ((), ()))
    vis_re = lax.dot_general(left_re, right_re, dims, preferred_element_type=jnp.float32)
    vis_re = vis_re + lax.dot_general(left_im, right_im, dims, preferred_element_type=jnp.float32)
    vis_im = lax.dot_general(left_im, right_re, dims, preferred_element_type=jnp.float32)
    vis_im = vis_im - lax.dot_general(left_re, right_im, dims, preferred_element_type=jnp.float32)
    return jnp.stack([vis_re, vis_im]) / frame_count


def correlate(left_view, right_view, frame_count):
    result = lax.map(
        lambda items: correlate_one(items[0], items[1], frame_count), (left_view, right_view)
    )
    return jnp.transpose(result, (1, 0, 2, 3))


def beams_one(weights, block):
    w_real = weights[0]
    w_imag = weights[1]
    x_real = block[0]
    x_imag = block[1]
    beam_re = jnp.dot(w_real, x_real, preferred_element_type=jnp.float32) - jnp.dot(
        w_imag, x_imag, preferred_element_type=jnp.float32
    )
    beam_im = jnp.dot(w_real, x_imag, preferred_element_type=jnp.float32) + jnp.dot(
        w_imag, x_real, preferred_element_type=jnp.float32
    )
    return jnp.stack([beam_re, beam_im], axis=1)


def form_beams(weights, view):
    by_channel = jnp.transpose(weights, (1, 0, 2, 3))
    return lax.map(lambda items: beams_one(items[0], items[1]), (by_channel, view))


def integrate(voltage):
    power = voltage[:, :, 0] * voltage[:, :, 0] + voltage[:, :, 1] * voltage[:, :, 1]
    return power.reshape(power.shape[0], power.shape[1], -1, INTEG).mean(axis=-1)


def channelize(voltages, input_flags, channel_order):
    masked = voltages * input_flags.astype(jnp.bfloat16)[None, :, None]
    local_inputs = masked.shape[1]
    frames = masked.shape[2] // NCH
    history = passed_along(masked[:, :, masked.shape[2] - (TAPS - 1) * NCH :], ("row", "col"), 1)
    joined = jnp.concatenate([history, masked], axis=2)
    blocks = joined.reshape(2, local_inputs, frames + TAPS - 1, NCH)
    coeffs = prototype(TAPS, NCH)
    filtered = jnp.zeros((2, local_inputs, frames, NCH), jnp.float32)
    for tap_index in range(TAPS):
        filtered = filtered + coeffs[tap_index] * blocks[
            :, :, tap_index : tap_index + frames
        ].astype(jnp.float32)
    filtered = filtered.astype(jnp.bfloat16)
    tables = dft_tables(channel_order, NCH)
    spectrum = jnp.einsum(
        "kqpn,pifn->kiqf",
        tables.astype(jnp.float32),
        filtered.astype(jnp.float32),
        precision=lax.Precision.HIGHEST,
    ).astype(jnp.bfloat16)
    spectrum = spectrum.reshape(NCH, local_inputs, 2 * frames)
    return spectrum


def by_panels(voltages, input_flags, channel_order, beam_weights):
    spectrum = channelize(voltages, input_flags, channel_order)
    frames = spectrum.shape[2] // 2
    turned = lax.all_to_all(spectrum, "chan", split_axis=0, concat_axis=1, tiled=True)
    row_count = lax.axis_size("row")
    col_count = lax.axis_size("col")
    total_frames = frames * row_count * col_count
    row_turned = lax.all_to_all(turned, "row", split_axis=1, concat_axis=2, tiled=True)
    row_all = lax.all_gather(row_turned, "col", axis=2, tiled=True)
    col_turned = lax.all_to_all(turned, "col", split_axis=1, concat_axis=2, tiled=True)
    col_all = lax.all_gather(col_turned, "row", axis=2, tiled=True)
    row_view = to_frames(row_all, frames, col_count, row_count, True)
    col_view = to_frames(col_all, frames, row_count, col_count, False)
    visibility = correlate(row_view, col_view, total_frames)
    weights_all = lax.all_gather(beam_weights, "col", axis=2, tiled=True)
    local_view = to_frames(turned, frames, 1, 1, False)
    voltage = form_beams(weights_all, local_view)
    own_power = integrate(voltage)
    beam_power = lax.all_to_all(own_power, "col", split_axis=1, concat_axis=2, tiled=True)
    return (visibility, beam_power)


MESH = pl.DeviceIdType.MESH


def spectra_tile(v_ref, h_ref, flag_ref, coeff_ref, table_ref, filtered_ref, wide_ref):
    tile = v_ref.shape[1]
    frames = v_ref.shape[2] // NCH
    lanes = 2 * frames
    flag = jnp.broadcast_to(flag_ref[...].astype(jnp.float32), (tile, NCH))
    rows = [jnp.broadcast_to(coeff_ref[tap : tap + 1, :], (tile, NCH)) for tap in range(TAPS)]
    for part in range(2):

        def frame_at(index):
            ref, at = (h_ref, index) if index < TAPS - 1 else (v_ref, index - TAPS + 1)
            return ref[part, :, at * NCH : (at + 1) * NCH].astype(jnp.float32) * flag

        window = [frame_at(index) for index in range(TAPS - 1)]
        for frame in range(frames):
            window = window[-(TAPS - 1) :] + [frame_at(frame + TAPS - 1)]
            total = rows[0] * window[0]
            for tap in range(1, TAPS):
                total = total + rows[tap] * window[tap]
            filtered_ref[part, frame] = total
    for first in range(0, tile, 2):
        stack = []
        for index in (first, first + 1):
            re = filtered_ref[0, :, index, :].astype(jnp.bfloat16)
            im = filtered_ref[1, :, index, :].astype(jnp.bfloat16)
            stack.append(jnp.concatenate([re, im], axis=1))
            stack.append(jnp.concatenate([im, -re], axis=1))
        both = lax.dot_general(
            table_ref[...],
            jnp.concatenate(stack, axis=0),
            (((1,), (1,)), ((), ())),
            preferred_element_type=jnp.float32,
        )
        wide_ref[:, first, :] = both[:, :lanes]
        wide_ref[:, first + 1, :] = both[:, lanes:]
    return wide_ref[...].astype(jnp.bfloat16)


def sizes():
    return lax.axis_size("chan"), lax.axis_size("row"), lax.axis_size("col")


def part_of(c, r, q, cs, half, qs, step):
    inner = step // cs
    row = r // half * half + (r % half + inner % half) % half
    return (c + step % cs) % cs, row, (q + inner // half) % qs


def turn_kernel(
    cs, rs, qs, tile, group, wide, alone, early,
    v_ref, flag_ref, coeff_ref, table_ref, whole_ref, x_ref, e_ref, s_ref,
    filtered_ref, wide_ref, spec_ref, past_ref, send, recv, psend, precv, local,
):
    c, r, q = (lax.axis_index(name) for name in ("chan", "row", "col"))
    half = rs // 2
    cells = rs * qs
    halves = half * qs
    devices = cs * cells
    me = r * qs + q
    mine = me % halves
    here = c * cells + me
    inputs = spec_ref.shape[1]
    lanes = spec_ref.shape[2]
    early_base = devices * alone
    late_base = early_base + cs * halves * early
    turn_step = pl.program_id(0)
    tiles = inputs // tile

    def ahead(step):
        return (r + step % rs) % rs * qs + (q + step // rs) % qs

    def rows_at(first, count):
        return pl.ds(pl.multiple_of(first, tile), count)

    def spectra(step, first, count):
        chan, cell = (c + step % cs) % cs, ahead(step // cs)
        origin, column = c, me
        return pltpu.make_async_remote_copy(
            src_ref=spec_ref.at[
                pl.ds((chan * cells + cell) * alone, alone), rows_at(first, count)
            ],
            dst_ref=x_ref.at[
                :,
                rows_at(origin * inputs + first, count),
                pl.ds(pl.multiple_of(column * lanes, lanes), lanes),
            ],
            send_sem=send.at[0],
            recv_sem=recv.at[0],
            device_id=(chan, cell // qs, cell % qs),
            device_id_type=MESH,
        )

    def sooner(step, first, count):
        chan, row, col = part_of(c, r, q, cs, half, qs, step)
        place = row % half * qs + col
        origin, column = c, mine
        return pltpu.make_async_remote_copy(
            src_ref=spec_ref.at[
                pl.ds(early_base + (chan * halves + place) * early, early), rows_at(first, count)
            ],
            dst_ref=e_ref.at[
                :,
                rows_at(origin * inputs + first, count),
                pl.ds(pl.multiple_of(column * lanes, lanes), lanes),
            ],
            send_sem=send.at[1],
            recv_sem=recv.at[1],
            device_id=(chan, row, col),
            device_id_type=MESH,
        )

    past = past_ref.shape[2]
    chunk = tile if inputs % wide else wide

    def last_frames(first):
        following = (me + 1) % cells
        rows = rows_at(first, chunk)
        return pltpu.make_async_remote_copy(
            src_ref=whole_ref.at[:, rows, pl.ds(whole_ref.shape[2] - past, past)],
            dst_ref=past_ref.at[:, rows],
            send_sem=psend.at[0],
            recv_sem=precv.at[first // chunk],
            device_id=(c, following // qs, following % qs),
            device_id_type=MESH,
        )

    @pl.when((turn_step == 0) & (me + 1 < cells))
    def _():
        for first in range(0, inputs, chunk):
            last_frames(first).start()

    @pl.when((turn_step == 0) & (me == 0))
    def _():
        past_ref[...] = jnp.zeros_like(past_ref)

    @pl.when((turn_step < tiles) & (me > 0) & (turn_step * tile % chunk == 0))
    def _():
        last_frames(turn_step * tile).wait_recv()

    @pl.when((turn_step == tiles) & (me + 1 < cells))
    def _():
        pltpu.make_async_remote_copy(
            src_ref=past_ref,
            dst_ref=past_ref,
            send_sem=psend.at[0],
            recv_sem=precv.at[0],
            device_id=(c, r, q),
            device_id_type=MESH,
        ).wait_send()

    @pl.when((turn_step > 0) & (turn_step * tile % group == 0))
    def _():
        def start(step, carry):
            spectra(step, turn_step * tile - group, group).start()
            return carry

        lax.fori_loop(1, devices, start, 0)

    @pl.when((turn_step > 0) & (turn_step * tile % wide == 0))
    def _():
        def start(step, carry):
            sooner(step, turn_step * tile - wide, wide).start()
            return carry

        lax.fori_loop(1, cs * halves, start, 0)

    @pl.when(turn_step < tiles)
    def _():
        at = pl.ds(pl.multiple_of(turn_step * tile, tile), tile)
        spec_ref[:, at, :] = spectra_tile(
            v_ref, past_ref.at[:, at], flag_ref, coeff_ref, table_ref, filtered_ref, wide_ref
        )

    @pl.when(turn_step == tiles)
    def _():
        stays = [
            pltpu.make_async_copy(
                spec_ref.at[pl.ds(here * alone, alone)],
                x_ref.at[
                    :, rows_at(c * inputs, inputs), pl.ds(pl.multiple_of(me * lanes, lanes), lanes)
                ],
                local.at[0],
            ),
            pltpu.make_async_copy(
                spec_ref.at[pl.ds(early_base + (c * halves + mine) * early, early)],
                e_ref.at[
                    :,
                    rows_at(c * inputs, inputs),
                    pl.ds(pl.multiple_of(mine * lanes, lanes), lanes),
                ],
                local.at[1],
            ),
            pltpu.make_async_copy(
                spec_ref.at[pl.ds(late_base, s_ref.shape[0])], s_ref, local.at[2]
            ),
        ]
        for stay in stays:
            stay.start()

        for index, count in enumerate(((devices - 1) * alone, (cs * halves - 1) * early)):
            rows = spec_ref.at[pl.ds(0, count)]
            every = pltpu.make_async_remote_copy(
                src_ref=rows,
                dst_ref=rows,
                send_sem=send.at[index],
                recv_sem=recv.at[index],
                device_id=(c, r, q),
                device_id_type=MESH,
            )
            every.wait_send()
            every.wait_recv()
        for stay in stays:
            stay.wait()


def turn(voltages, input_flags, channel_order, alone, shared, early):
    cs, rs, qs = sizes()
    devices = cs * rs * qs
    halves = rs // 2 * qs
    _, inputs, samples = voltages.shape
    past = (TAPS - 1) * NCH
    frames = samples // NCH
    lanes = 2 * frames
    tile = 16
    group = tile
    wide = 4 * group if inputs % (4 * group) == 0 else group
    last = inputs // tile - 1
    place = channel_order.reshape(cs, NCH // cs)
    split = place[:, rs * qs * alone :].reshape(cs, halves, shared)
    order = jnp.concatenate(
        [
            place[:, : rs * qs * alone].reshape(-1),
            split[:, :, :early].reshape(-1),
            split[:, :, early:].reshape(-1),
        ]
    )
    tables = dft_tables(order, NCH)[:, 0].reshape(NCH, 2 * NCH)
    anywhere = pl.BlockSpec(memory_space=pl.ANY)
    counts = (2, 2, 1, inputs // tile, 3)
    return pl.pallas_call(
        functools.partial(turn_kernel, cs, rs, qs, tile, group, wide, alone, early),
        grid=(inputs // tile + 1,),
        out_shape=(
            jax.ShapeDtypeStruct((alone, inputs * cs, lanes * rs * qs), jnp.bfloat16),
            jax.ShapeDtypeStruct((early, inputs * cs, lanes * halves), jnp.bfloat16),
            jax.ShapeDtypeStruct((cs * halves * (shared - early), inputs, lanes), jnp.bfloat16),
        ),
        in_specs=[
            pl.BlockSpec((2, tile, samples), lambda i: (0, jnp.minimum(i, last), 0)),
            pl.BlockSpec((tile, 1), lambda i: (jnp.minimum(i, last), 0)),
            pl.BlockSpec((TAPS, NCH), lambda i: (0, 0)),
            pl.BlockSpec((NCH, 2 * NCH), lambda i: (0, 0)),
            anywhere,
        ],
        out_specs=(anywhere,) * 3,
        scratch_shapes=[
            pltpu.VMEM((2, frames, tile, NCH), jnp.float32),
            pltpu.VMEM((NCH, tile, lanes), jnp.float32),
            pltpu.VMEM((NCH, inputs, lanes), jnp.bfloat16),
            pltpu.VMEM((2, inputs, past), jnp.bfloat16),
        ]
        + [pltpu.SemaphoreType.DMA((count,)) for count in counts],
        compiler_params=pltpu.CompilerParams(has_side_effects=True, vmem_limit_bytes=60 << 20),
        name="turn",
    )(
        voltages,
        input_flags[:, None],
        jnp.asarray(prototype_values(TAPS, NCH), jnp.float32),
        tables,
        voltages,
    )


def crosses(half, source_row, row, col):
    return (row != col) & (row // half == col // half) & (source_row // half != row // half)


def nearer(half, row, col):
    upper = row // half == 1
    return (upper & (row < col)) | (jnp.logical_not(upper) & (row > col))


def mirrored(half, source_row, row, col):
    return crosses(half, source_row, row, col) & jnp.logical_not(nearer(half, row, col))


def products_kernel(
    cs, rs, qs, frame_count, alone, early,
    xa_ref, xe_ref, s_ref, weight_ref, swap_ref, pool_ref,
    block_ref, parta_ref, partb_ref, late_ref, all_ref, stage_ref,
    x_ref, y_ref, w_ref, vis_ref, powera_ref, powerb_ref,
    load, send, recv, stage_send, stage_recv, relay_send,
    psend, precv, lsend, lrecv, wsend, wrecv, wload, local,
):
    c, r, q = (lax.axis_index(name) for name in ("chan", "row", "col"))
    cells = rs * qs
    half = rs // 2
    halves = half * qs
    me = r * qs + q
    mine = me % halves
    held, inputs = vis_ref.shape[1], vis_ref.shape[2]
    shared = held - alone
    late = shared - early
    depth = x_ref.shape[2]
    depths = {False: depth, True: depth // 2}
    lanes = swap_ref.shape[0]
    own_inputs = inputs // cs
    height, width = block_ref.shape[2], block_ref.shape[3]
    part_height, part_width = parta_ref.shape[1], parta_ref.shape[2]
    now = pl.program_id(0)

    def ahead(step, sign):
        row = (r + rs + sign * (step % rs)) % rs
        return row * qs + (q + qs + sign * (step // rs)) % qs

    def vis_at(planes, first, count, row, col):
        return vis_ref.at[
            pl.ds(0, planes),
            pl.ds(first, count),
            pl.ds(pl.multiple_of(row * height, height), height),
            pl.ds(pl.multiple_of(col * width, width), width),
        ]

    def power_at(ref, row, col):
        return ref.at[
            pl.ds(pl.multiple_of(col * part_height, part_height), part_height),
            pl.ds(pl.multiple_of(row * part_width, part_width), part_width),
        ]

    def landing(kind, planes, cell, first, count):
        base = cells * alone + cell * shared if kind else cell * alone
        return block_ref.at[pl.ds(0, planes), pl.ds(base + first, count)]

    def outgoing(kind, planes, cell, first, count):
        return pltpu.make_async_remote_copy(
            src_ref=vis_at(planes, first + (alone if kind else 0), count, cell // qs, cell % qs),
            dst_ref=landing(kind, planes, me, first, count),
            send_sem=send.at[planes - 1],
            recv_sem=recv.at[0],
            device_id=(c, cell // qs, cell % qs),
            device_id_type=MESH,
        )

    def together(rows, leaves, comes):
        return pltpu.make_async_remote_copy(
            src_ref=rows,
            dst_ref=rows,
            send_sem=leaves,
            recv_sem=comes,
            device_id=(c, r, q),
            device_id_type=MESH,
        )

    def staged(pair, row, first, count):
        return stage_ref.at[:, pl.ds((pair * half + row % half) * held + first, count)]

    def to_relay(row, col, first, count):
        inner = jnp.where(r < half, row - half, half - 1 - row)
        outer = jnp.where(r < half, col - half, half - 1 - col)
        pair = inner * (2 * half - inner - 1) // 2 + outer - inner - 1
        return pltpu.make_async_remote_copy(
            src_ref=vis_at(2, first, count, row, col),
            dst_ref=staged(pair, r, first, count),
            send_sem=stage_send.at[0],
            recv_sem=stage_recv.at[(pair * half + r % half) * held + first],
            device_id=(c, jnp.where(r < half, half, half - 1), q),
            device_id_type=MESH,
        )

    def at_relay(pair, row, first):
        return pltpu.make_async_remote_copy(
            src_ref=staged(pair, row, first, 1),
            dst_ref=staged(pair, row, first, 1),
            send_sem=stage_send.at[0],
            recv_sem=stage_recv.at[(pair * half + row % half) * held + first],
            device_id=(c, row, q),
            device_id_type=MESH,
        )

    def from_relay(kind, pair, row, at, first, count, goal):
        return pltpu.make_async_remote_copy(
            src_ref=staged(pair, row, first, count),
            dst_ref=landing(kind, 2, row * qs + q, at, count),
            send_sem=relay_send.at[0],
            recv_sem=recv.at[0],
            device_id=(c,) + goal,
            device_id_type=MESH,
        )

    relays = r == jnp.where(r < half, half - 1, half)
    pairs = [(inner, outer) for inner in range(half) for outer in range(inner + 1, half)]

    def owners(pair):
        inner, outer = pairs[pair]
        row = jnp.where(r < half, half - 1 - inner, half + inner)
        col = jnp.where(r < half, half - 1 - outer, half + outer)
        return row, col

    def both(diagonal, sent, act):
        @pl.when(sent & diagonal)
        def _():
            act(1)

        @pl.when(sent & jnp.logical_not(diagonal))
        def _():
            act(2)

    def part(kind, cell, slot):
        source, goal = (powerb_ref, partb_ref) if kind else (powera_ref, parta_ref)
        row = cell // qs % half if kind else cell // qs
        place = slot % halves if kind else slot
        return pltpu.make_async_remote_copy(
            src_ref=power_at(source, row, cell % qs),
            dst_ref=goal.at[place],
            send_sem=psend.at[1 if kind else 0],
            recv_sem=precv.at[1 if kind else 0],
            device_id=(c, cell // qs, cell % qs),
            device_id_type=MESH,
        )

    peers = cs * halves

    def spread(step, at):
        chan, row, col = part_of(c, r, q, cs, half, qs, step)
        place = row % half * qs + col
        origin, column = c, mine
        return pltpu.make_async_remote_copy(
            src_ref=s_ref.at[(chan * halves + place) * late + at],
            dst_ref=late_ref.at[
                at,
                pl.ds(pl.multiple_of(origin * own_inputs, own_inputs), own_inputs),
                pl.ds(pl.multiple_of(column * lanes, lanes), lanes),
            ],
            send_sem=lsend.at[0],
            recv_sem=lrecv.at[at],
            device_id=(chan, row, col),
            device_id_type=MESH,
        )

    def stay_late(at):
        return pltpu.make_async_copy(
            s_ref.at[(c * halves + mine) * late + at],
            late_ref.at[
                at,
                pl.ds(pl.multiple_of(c * own_inputs, own_inputs), own_inputs),
                pl.ds(pl.multiple_of(mine * lanes, lanes), lanes),
            ],
            local.at[4],
        )

    def fetch(source, slot, kind):
        return pltpu.make_async_copy(
            source, x_ref.at[slot, :, pl.ds(0, depths[kind])], load.at[slot]
        )

    def weight_spans(peer):
        cell = r * qs + peer
        return (
            (cell * alone, 0, alone),
            (cells * alone + cell % halves * shared, alone, shared),
        )

    def weights_at(slot, goal, count):
        beams = weight_ref.shape[2]
        return all_ref.at[
            :, pl.ds(goal, count), pl.ds(pl.multiple_of(slot * beams, beams), beams)
        ]

    def weights(peer, slot, source, goal, count):
        return pltpu.make_async_remote_copy(
            src_ref=weight_ref.at[:, pl.ds(source, count)],
            dst_ref=weights_at(slot, goal, count),
            send_sem=wsend.at[peer],
            recv_sem=wrecv.at[slot],
            device_id=(c, r, peer),
            device_id_type=MESH,
        )

    keeps = [
        pltpu.make_async_copy(
            weight_ref.at[:, pl.ds(source, count)], weights_at(q, goal, count), local.at[5 + index]
        )
        for index, (source, goal, count) in enumerate(weight_spans(q))
    ]

    def fetch_weights(index, slot):
        return pltpu.make_async_copy(all_ref.at[:, index], w_ref.at[slot], wload.at[slot])

    def visibility_of(kind, slot, at):
        deep = depths[kind]
        across = (((1,), (1,)), ((), ()))
        index = at + (alone if kind else 0)

        def panels(step, carry):
            col = (q + step) % qs
            span = pl.ds(pl.multiple_of(col * width, width), width)
            for start in range(0, deep, lanes):
                y_ref[:, start : start + lanes] = jnp.dot(
                    x_ref[slot, span, start : start + lanes],
                    swap_ref[...],
                    preferred_element_type=jnp.float32,
                ).astype(jnp.bfloat16)
            every = x_ref[slot, :, :deep]
            re = lax.dot_general(
                every, x_ref[slot, span, :deep], across, preferred_element_type=jnp.float32
            )
            im = lax.dot_general(every, y_ref[:, :deep], across, preferred_element_type=jnp.float32)
            panel = lax.broadcasted_iota(jnp.int32, re.shape, 0) // height
            first = jnp.where(panel == col, re + im, re)
            vis_ref[0, index, :, span] = (first / frame_count).astype(vis_ref.dtype)
            vis_ref[1, index, :, span] = (im / frame_count).astype(vis_ref.dtype)

            def start(step, carry):
                outward = jnp.where(step % 2 == 0, half + step // 2, half - 1 - step // 2)
                row = jnp.where(r < half, outward, rs - 1 - outward)
                cell = row * qs + col
                shared_pair = crosses(half, r, row, col)
                sent = (cell != me) & jnp.logical_not(shared_pair)
                both(row == col, sent, lambda planes: outgoing(kind, planes, cell, at, 1).start())

                @pl.when(shared_pair & nearer(half, row, col))
                def _():
                    to_relay(row, col, index, 1).start()

                return carry

            lax.fori_loop(0, rs, start, 0)
            return carry

        lax.fori_loop(0, qs, panels, 0)

    def beams_of(kind, slot, at):
        deep = depths[kind]
        span = 4 * lanes if deep % (4 * lanes) == 0 else lanes
        power_ref = powerb_ref if kind else powera_ref
        columns_out = power_ref.shape[1]
        middle = lanes // 2

        def columns(step, carry):
            along = pl.ds(pl.multiple_of(step * span, span), span)
            x = x_ref[slot, :, along]
            straight = jnp.dot(w_ref[slot, 0], x, preferred_element_type=jnp.float32)
            crossed = jnp.dot(w_ref[slot, 1], x, preferred_element_type=jnp.float32)
            swapped = []
            for start in range(0, span, lanes):
                swapped.append(crossed[:, start + middle : start + lanes])
                swapped.append(-crossed[:, start : start + middle])
            beam = straight - jnp.concatenate(swapped, axis=1)
            square = beam * beam
            high = square.astype(jnp.bfloat16)
            low = (square - high.astype(jnp.float32)).astype(jnp.bfloat16)
            pool = pool_ref[along, :columns_out]
            return (
                carry
                + jnp.dot(high, pool, preferred_element_type=jnp.float32)
                + jnp.dot(low, pool, preferred_element_type=jnp.float32)
            )

        found = lax.fori_loop(0, deep // span, columns, jnp.zeros(power_ref.shape, jnp.float32))
        lane = lax.broadcasted_iota(jnp.int32, power_ref.shape, 1) % part_width
        kept = power_ref[...].astype(jnp.float32)
        kept = jnp.where(lane // (part_width // shared) == at, found, kept)
        power_ref[...] = kept.astype(power_ref.dtype)

    def pass_on(kind, at):
        index = at + (alone if kind else 0)

        @pl.when(relays)
        def _():
            for pair in range(len(pairs)):
                row, col = owners(pair)

                def one(step, carry, pair=pair, row=row, col=col):
                    source = (1 - r // half) * half + step
                    at_relay(pair, source, index).wait_recv()
                    from_relay(kind, pair, source, at, index, 1, (col, row)).start()
                    mine_too = (row == r) & (col == q)

                    @pl.when(mine_too)
                    def _():
                        pltpu.make_async_copy(
                            staged(pair, source, index, 1),
                            landing(kind, 2, source * qs + q, at, 1),
                            recv.at[0],
                        ).start()

                    @pl.when(jnp.logical_not(mine_too))
                    def _():
                        from_relay(kind, pair, source, at, index, 1, (row, col)).start()

                    return carry

                lax.fori_loop(0, half, one, 0)

    locals_ = [
        pltpu.make_async_copy(
            vis_at(2, 0, alone, r, q), landing(False, 2, me, 0, alone), local.at[0]
        ),
        pltpu.make_async_copy(
            vis_at(2, alone, shared, r, q), landing(True, 2, me, 0, shared), local.at[1]
        ),
        pltpu.make_async_copy(power_at(powera_ref, r, q), parta_ref.at[me], local.at[2]),
        pltpu.make_async_copy(power_at(powerb_ref, r % half, q), partb_ref.at[mine], local.at[3]),
    ]
    coming = (now + 1) % held
    next_slot = (now + 1) % 2
    more = now + 1 < 2 * held
    turn_index = now % held

    @pl.when(now == 0)
    def _():
        powera_ref[...] = jnp.zeros_like(powera_ref)
        powerb_ref[...] = jnp.zeros_like(powerb_ref)
        fetch(xa_ref.at[0], 0, False).start()

    @pl.when(now < late)
    def _():
        def start(step, carry):
            spread(step, now).start()
            return carry

        lax.fori_loop(1, cs * halves, start, 0)
        stay = stay_late(now)
        stay.start()
        stay.wait()

    @pl.when(now == late)
    def _():
        def start(step, carry):
            peer = (q + step) % qs
            for source, goal, count in weight_spans(peer):
                weights(peer, q, source, goal, count).start()
            return carry

        lax.fori_loop(1, qs, start, 0)
        for keep in keeps:
            keep.start()

    @pl.when(more & (coming < alone))
    def _():
        fetch(xa_ref.at[coming], next_slot, False).start()

    @pl.when(more & (coming >= alone) & (coming < alone + early))
    def _():
        fetch(xe_ref.at[coming - alone], next_slot, True).start()

    @pl.when(now == held)
    def _():
        def arrive(step, carry):
            behind = (q + qs - step) % qs
            weights(behind, behind, 0, 0, held).wait_recv()
            return carry

        lax.fori_loop(1, qs, arrive, 0)
        for keep in keeps:
            keep.wait()
        fetch_weights(0, held % 2).start()

    @pl.when((now >= held) & more)
    def _():
        fetch_weights(coming, next_slot).start()

    @pl.when((now < 2 * held) & (turn_index < alone))
    def _():
        fetch(xa_ref.at[0], now % 2, False).wait()

        @pl.when(now < held)
        def _():
            visibility_of(False, now % 2, turn_index)

        @pl.when(now >= held)
        def _():
            fetch_weights(0, now % 2).wait()
            beams_of(False, now % 2, turn_index)
            pass_on(False, turn_index)

    @pl.when((now < 2 * held) & (turn_index >= alone))
    def _():
        fetch(xe_ref.at[0], now % 2, True).wait()

        @pl.when(now < held)
        def _():
            visibility_of(True, now % 2, turn_index - alone)

        @pl.when(now >= held)
        def _():
            fetch_weights(0, now % 2).wait()
            beams_of(True, now % 2, turn_index - alone)

        @pl.when(now == 2 * held - 1)
        def _():
            def start(step, carry):
                cell = ahead(step, 1)
                part(False, cell, me).start()

                @pl.when(cell // halves == r // half)
                def _():
                    part(True, cell, me).start()

                return carry

            lax.fori_loop(1, cells, start, 0)
            for copy in locals_:
                copy.start()

        @pl.when(now >= held)
        def _():
            pass_on(True, turn_index - alone)

    @pl.when(more & (coming >= alone + early))
    def _():
        at = coming - alone - early

        @pl.when(now < held)
        def _():
            together(s_ref.at[pl.ds(0, peers - 1)], lsend.at[0], lrecv.at[at]).wait_recv()

        fetch(late_ref.at[at], next_slot, True).start()

    @pl.when(now == 2 * held)
    def _():
        plain = cells - 1 - rs - 2 * len(pairs)

        def sent(diagonal, straight):
            for planes, count in ((1, diagonal), (2, straight)):
                rows = block_ref.at[pl.ds(0, planes), pl.ds(0, count * held)]
                together(rows, send.at[planes - 1], recv.at[0]).wait_send()

        @pl.when(r == q)
        def _():
            sent(rs - 1, plain + 1)
            rows = block_ref.at[pl.ds(0, 1), pl.ds(0, (cells - 1) * held)]
            together(rows, send.at[0], recv.at[0]).wait_recv()

        @pl.when(r != q)
        def _():
            sent(rs, plain)
            rows = block_ref.at[pl.ds(0, 2), pl.ds(0, (cells - 1) * held)]
            together(rows, send.at[0], recv.at[0]).wait_recv()

        rows = block_ref.at[pl.ds(0, 2), pl.ds(0, len(pairs) * held)]
        together(rows, stage_send.at[0], recv.at[0]).wait_send()
        for index, (ref, count) in enumerate(((parta_ref, cells - 1), (partb_ref, halves - 1))):
            every = together(ref.at[pl.ds(0, count)], psend.at[index], precv.at[index])
            every.wait_send()
            every.wait_recv()

        @pl.when(relays)
        def _():
            own = jnp.where(r < half, r > q, r < q) & (r // half == q // half)
            all_passed = 2 * len(pairs) * half * held

            def passed(count):
                rows = block_ref.at[pl.ds(0, 2), pl.ds(0, count)]
                together(rows, relay_send.at[0], recv.at[0]).wait_send()

            @pl.when(own)
            def _():
                passed(all_passed - half * held)

            @pl.when(jnp.logical_not(own))
            def _():
                passed(all_passed)

        together(s_ref.at[pl.ds(0, late * (peers - 1))], lsend.at[0], lrecv.at[0]).wait_send()

        def sent_weights(step, carry):
            weights((q + step) % qs, q, 0, 0, held).wait_send()
            return carry

        lax.fori_loop(1, qs, sent_weights, 0)
        for copy in locals_:
            copy.wait()


def products(xa, xe, rest, weights, frames, shared):
    cs, rs, qs = sizes()
    cells = rs * qs
    halves = cells // 2
    alone, inputs, depth = xa.shape
    early = xe.shape[0]
    late = shared - early
    held = alone + shared
    beams = weights.shape[2] * qs
    bins = depth // (2 * INTEG)
    lanes = 2 * frames
    source = np.arange(lanes)[:, None]
    goal = np.arange(lanes)[None, :]
    swap = np.where(source + frames == goal, 1.0, 0.0) - np.where(source == goal + frames, 1.0, 0.0)
    at = np.arange(depth)
    frame = at // lanes * frames + at % frames
    part = bins // rs
    column = np.arange(rs * shared * part)
    bin_of = column // (shared * part) * part + column % part
    pool = np.where(frame[:, None] // INTEG == bin_of[None, :], 1.0 / INTEG, 0.0)
    anywhere = pl.BlockSpec(memory_space=pl.ANY)
    half = rs // 2
    pairs = half * (half - 1) // 2
    stages = pairs * half * held
    counts = (2, 2, 1, 1, stages, 1, 2, 2, 1, late, qs, qs, 2, 7)
    return pl.pallas_call(
        functools.partial(products_kernel, cs, rs, qs, depth // 2, alone, early),
        grid=(2 * held + 1,),
        out_shape=(
            jax.ShapeDtypeStruct((2, cells * held, inputs // rs, inputs // qs), jnp.bfloat16),
            jax.ShapeDtypeStruct((cells, beams // qs, shared * part), jnp.bfloat16),
            jax.ShapeDtypeStruct((halves, beams // qs, shared * part), jnp.bfloat16),
            jax.ShapeDtypeStruct((late, inputs, depth // 2), jnp.bfloat16),
            jax.ShapeDtypeStruct((2, held, beams, inputs), weights.dtype),
            jax.ShapeDtypeStruct((2, stages, inputs // rs, inputs // qs), jnp.bfloat16),
        ),
        in_specs=[
            anywhere,
            anywhere,
            anywhere,
            anywhere,
            pl.BlockSpec((lanes, lanes), lambda j: (0, 0)),
            pl.BlockSpec((depth, rs * shared * part), lambda j: (0, 0)),
        ],
        out_specs=(anywhere,) * 6,
        scratch_shapes=[
            pltpu.VMEM((2, inputs, depth), jnp.bfloat16),
            pltpu.VMEM((inputs // qs, depth), jnp.bfloat16),
            pltpu.VMEM((2, 2, beams, inputs), weights.dtype),
            pltpu.VMEM((2, held, inputs, inputs), jnp.bfloat16),
            pltpu.VMEM((beams, rs * shared * part), jnp.bfloat16),
            pltpu.VMEM((beams, rs // 2 * shared * part), jnp.bfloat16),
        ]
        + [pltpu.SemaphoreType.DMA((count,)) for count in counts],
        compiler_params=pltpu.CompilerParams(has_side_effects=True, vmem_limit_bytes=60 << 20),
        name="products",
    )(xa, xe, rest, weights, jnp.asarray(swap, jnp.bfloat16), jnp.asarray(pool, jnp.bfloat16))


def unpack_kernel(
    rs, qs, singles, part, one_ref, two_ref, parta_ref, partb_ref, eye_ref, out_ref, power_ref
):
    r, q = (lax.axis_index(name) for name in ("row", "col"))
    half = rs // 2
    step = pl.program_id(0)
    summed = step >= singles

    def turned(value):
        return lax.dot_general(
            eye_ref[...], value, (((1,), (1,)), ((), ())), preferred_element_type=jnp.float32
        )

    def straight_pair(ref, at):
        return ref[0, at].astype(jnp.float32), ref[1, at].astype(jnp.float32)

    def turned_pair(ref, at):
        return turned(ref[0, at]), -turned(ref[1, at])

    def packed_pair(ref, at):
        wide, over = ref[0, at].astype(jnp.float32), turned(ref[0, at])
        return 0.5 * (wide + over), 0.5 * (wide - over)

    def put(when, *ways):
        @pl.when(when)
        def _():
            for at in range(out_ref.shape[1]):
                re, im = ways[0](one_ref, at)
                if len(ways) > 1:
                    more_re, more_im = ways[1](two_ref, at)
                    re, im = re + more_re, im + more_im
                out_ref[0, at] = re
                out_ref[1, at] = im

    single = jnp.logical_not(summed)

    def put_power(ref):
        each = power_ref.shape[0] // ref.shape[0]
        for source in range(ref.shape[0]):
            across = ref[source].astype(jnp.float32).T
            for at in range(each):
                power_ref[source * each + at] = across[at * part : (at + 1) * part]

    @pl.when(single)
    def _():
        put_power(parta_ref)

    @pl.when(summed)
    def _():
        put_power(partb_ref)

    off = r != q
    over = mirrored(half, step * rs // singles, r, q)
    put(single & (r == q), packed_pair)
    put(single & over, turned_pair)
    put(single & off & jnp.logical_not(over), straight_pair)
    low = mirrored(half, 0, r, q)
    high = mirrored(half, half, r, q)
    put(summed & (r == q), packed_pair, packed_pair)
    put(summed & low, turned_pair, straight_pair)
    put(summed & high, straight_pair, turned_pair)
    neither = jnp.logical_not(low) & jnp.logical_not(high)
    put(summed & off & neither, straight_pair, straight_pair)


def unpack(block, whole, halved, alone, shared):
    _, rs, qs = sizes()
    cells = rs * qs
    span = 2 * shared
    singles = cells * alone // span
    doubles = cells // 2 * shared // span
    _, _, height, width = block.shape
    _, beams, lanes = whole.shape
    part = lanes // shared
    steps = singles + doubles
    shape = (2, span, height, width)
    visibility, power = pl.pallas_call(
        functools.partial(unpack_kernel, rs, qs, singles, part),
        grid=(steps,),
        out_shape=(
            jax.ShapeDtypeStruct((2, steps * span, height, width), jnp.float32),
            jax.ShapeDtypeStruct((steps * span, part, beams), jnp.float32),
        ),
        in_specs=[
            pl.BlockSpec(shape, lambda i: (0, i, 0, 0)),
            pl.BlockSpec(shape, lambda i: (0, jnp.maximum(i, singles) + doubles, 0, 0)),
            pl.BlockSpec((span // alone, beams, lanes), lambda i: (jnp.minimum(i, singles - 1), 0, 0)),
            pl.BlockSpec((span // shared, beams, lanes), lambda i: (jnp.maximum(i - singles, 0), 0, 0)),
            pl.BlockSpec((height, width), lambda i: (0, 0)),
        ],
        out_specs=(
            pl.BlockSpec(shape, lambda i: (0, i, 0, 0)),
            pl.BlockSpec((span, part, beams), lambda i: (i, 0, 0)),
        ),
        compiler_params=pltpu.CompilerParams(vmem_limit_bytes=60 << 20),
        name="unpack",
    )(block, block, whole, halved, jnp.asarray(np.eye(height), jnp.bfloat16))
    return visibility, jnp.transpose(power, (0, 2, 1))


def by_channels(voltages, input_flags, channel_order, beam_weights):
    cs, rs, qs = sizes()
    own = NCH // (cs * rs * qs)
    alone, shared, early = own // 2, own, own // 2
    xa, xe, rest = turn(voltages, input_flags, channel_order, alone, shared, early)
    frames = voltages.shape[2] // NCH
    block, whole, halved = products(xa, xe, rest, beam_weights, frames, shared)[:3]
    return unpack(block, whole, halved, alone, shared)


def on_device(voltages, input_flags, channel_order, beam_weights):
    cs, rs, qs = sizes()
    lanes = 2 * (voltages.shape[2] // NCH)
    devices = cs * rs * qs
    square = rs == qs and rs % 2 == 0 and rs > 2 and NCH // devices % 2 == 0
    whole = square and NCH % devices == 0 and lanes % 128 == 0 and voltages.shape[1] % 16 == 0
    if whole and NCH // devices * (lanes // 2 * qs // INTEG) % 128 == 0:
        plan = by_channels
    else:
        plan = by_panels
    return plan(voltages, input_flags, channel_order, beam_weights)


def solution(mesh):
    placed = (P(None, "chan", ("row", "col")), P("chan"), P(), P(None, "chan", "col", None))
    return jax.shard_map(
        on_device,
        mesh=mesh,
        in_specs=placed,
        out_specs=(P(None, "chan", "row", "col"), P("chan", "col", "row")),
        check_vma=False,
    )
```
